32 devices in a mesh: grp: 2 (over y), tm: 4 (over z), row: 2 (over x), col: 2 (over core).
Axes of the slice: x: 2, y: 2, z: 4, core: 2. Of those that a mesh axis runs over, the one named last changes fastest.
Arguments:
- frames: bfloat16 [8, 16, 9216], P(('grp', 'tm'), 'row', 'col'), parts along dimension 0, may hold values from -6 to 6
- owner_map: int32 [8], P('grp'), parts along dimension 0, may hold values from 0 to 3, each once
- valid_blocks: int32 [8, 2, 36], P(('grp', 'tm'), 'row', 'col'), parts along dimension 0, may hold values 0 or 1
- deblock_weight: bfloat16 [288, 32], replicated, may hold values from -0.375 to 0.375
- deblock_bias: float32 [32], replicated, may hold values from -3 to 3
- encoder_weight: bfloat16 [864, 64], replicated, may hold values from -0.21875 to 0.21875
- encoder_bias: float32 [64], replicated, may hold values from -3 to 3
Outputs:
- encoded: bfloat16 [6, 2, 4, 9216], P('grp', 'row', 'tm', 'col'), parts along dimension 0
The draws below stay inside these ranges and needn't reach their ends.
There are 2 independent parts, one for each index of `grp`. The reference program is written for one: setup_inputs(seed, part) draws one part's arguments, and reference() takes and returns one part's arrays. A program takes and returns all parts, laid end to end along the dimension named above; an argument that names none is the same for every part. Nothing has to cross between parts.
Inputs may be any that keep to these rules, and one draw needn't show every extreme that they name: `owner_map`: each time index is held by exactly one slot.
All inputs are finite; a program needn't handle non-finite values. No bound on the sum of `valid_blocks` on one device may be relied on, other than what follows from the above.
Results may differ from the reference program's by a relative error of at most 0.0085.
Values may be sent and summed in bfloat16 or wider, within the bound.
No kernel may reach another device: no remote copies, remote signals or barrier semaphores. Data moves between devices by JAX's collectives and lax.ppermute only.
A program may use at most 64 MiB of HBM per device.

```python
import jax
import jax.numpy as jnp
from jax import lax

CH = 32
OUTC = 64
BAND = 1
ROWS = 16
COLS = 288
FRAMES = 4
OUT_FRAMES = 3
N_TM = 4
N_ROW = 2


def with_ends(array, stream_key, low, top_value):
    dims = array.shape
    spot = [jax.random.randint(jax.random.fold_in(stream_key, axis), (), 0, dims[axis]) for axis in range(len(dims))]
    array = array.at[tuple(spot)].set(low)
    longest = dims.index(max(dims))
    spot[longest] = (spot[longest] + 1) % dims[longest]
    return array.at[tuple(spot)].set(top_value)


def steps_of(key, shape, split, least, top_value):
    def one(position, shards_of):
        draws = jax.random.uniform(jax.random.fold_in(jax.random.fold_in(key, 6), position), (shards_of,), jnp.float32, least / len(split), top_value / len(split))
        return jnp.repeat(jnp.exp(draws), shape[position] // shards_of).reshape((-1,) + (1,) * (len(shape) - position - 1))

    level = one(*split[0])
    for cut in split[1:]:
        level = level * one(*cut)
    return level


def normal_values(own_key, shape, deviation, reach, split=(), held_as=jnp.bfloat16):
    level = steps_of(own_key, shape, split, -0.22, 0.18) if split else 1.0
    values = jax.random.normal(own_key, shape, jnp.float32) * deviation * level
    return jnp.minimum(jnp.maximum(values, -reach), reach).astype(held_as)


def setup_inputs(seed: int = 0, part: int = 0) -> dict:
    seeds = jax.random.split(jax.random.key(seed), 8)
    own_keys = jax.random.split(jax.random.fold_in(seeds[7], part), 8)
    return {
        "frames": normal_values(own_keys[0], (FRAMES, ROWS, COLS * CH), 1.0, 6.0, ((0, 4), (1, 2), (2, 2))),
        "owner_map": jax.random.permutation(own_keys[1], FRAMES).astype(jnp.int32),
        "valid_blocks": with_ends((jax.random.randint(own_keys[2], (FRAMES, ROWS // 8, COLS // 8), 0, 4) < 3).astype(jnp.int32), jax.random.fold_in(own_keys[2], 1), 0, 1),
        "deblock_weight": normal_values(seeds[3], (9 * CH, CH), (9 * CH) ** -0.5, 0.375),
        "deblock_bias": normal_values(seeds[4], (CH,), 0.5, 3.0, (), jnp.float32),
        "encoder_weight": normal_values(seeds[5], (27 * CH, OUTC), (27 * CH) ** -0.5, 0.21875),
        "encoder_bias": normal_values(seeds[6], (OUTC,), 0.5, 3.0, (), jnp.float32),
    }


def conv_taps(padded, weight, height, extent):
    channels = padded.shape[-1]
    summed = jnp.zeros((), jnp.float32)
    for row_step in range(3):
        stripe = padded[..., row_step:row_step + height, :, :]
        patches = jnp.concatenate([stripe[..., col_step:col_step + extent, :] for col_step in range(3)], axis=-1)
        patches = patches.reshape(-1, 3 * channels)
        kernel = weight[row_step * 3 * channels:(row_step + 1) * 3 * channels]
        summed = summed + jnp.dot(patches, kernel, preferred_element_type=jnp.float32)
    return summed


def pool_pairs(source):
    leading = source.shape[:-3]
    height, extent, channels = source.shape[-3:]
    grouped = source.astype(jnp.float32).reshape(leading + (height // 2, 2, extent // 2, 2, channels))
    depth = len(leading)
    return jnp.mean(grouped, axis=(depth + 1, depth + 3)).astype(jnp.bfloat16)


def reference(frames, owner_map, valid_blocks, deblock_weight, deblock_bias, encoder_weight, encoder_bias):
    def clean_one(item):
        frame, blocks = item
        image = frame.reshape(ROWS, COLS, CH)
        framed = jnp.pad(image, ((1, 1), (1, 1), (0, 0)))
        filtered = conv_taps(framed, deblock_weight, ROWS, COLS).reshape(ROWS, COLS, CH) + deblock_bias
        coverage = jnp.broadcast_to(blocks.astype(jnp.float32)[:, None, :, None], (ROWS // 8, 8, COLS // 8, 8)).reshape(ROWS, COLS, 1)
        cleaned = (image.astype(jnp.float32) + coverage * filtered).astype(jnp.bfloat16)
        return pool_pairs(cleaned)

    pooled = lax.map(clean_one, (frames, valid_blocks))
    indices = jnp.arange(FRAMES, dtype=jnp.int32)
    matches = (owner_map[None, :] == indices[:, None]).astype(jnp.int32)
    slot_of_time = jnp.sum(matches * indices[None, :], axis=1).astype(jnp.int32)
    ordered = jnp.take(pooled, slot_of_time, axis=0)

    def encode_one(output_index):
        moment = output_index + 1
        summed = jnp.zeros(((ROWS // 2) * (COLS // 2), OUTC), jnp.float32)
        for frame_lag in range(3):
            chosen = jnp.maximum(moment - frame_lag, 0).astype(jnp.int32)
            picture = lax.dynamic_index_in_dim(ordered, chosen, 0, keepdims=False)
            framed = jnp.pad(picture, ((1, 1), (1, 1), (0, 0)))
            kernel = encoder_weight[frame_lag * 9 * CH:(frame_lag + 1) * 9 * CH]
            summed = summed + conv_taps(framed, kernel, ROWS // 2, COLS // 2)
        return (summed + encoder_bias).astype(jnp.bfloat16)

    encoded = lax.map(encode_one, jnp.arange(OUT_FRAMES, dtype=jnp.int32))
    return encoded.reshape(OUT_FRAMES, N_ROW, N_TM * BAND, (COLS // 2) * OUTC)
```

```python
import functools

import jax
import jax.numpy as jnp
from jax import lax
from jax.experimental import pallas as pl
from jax.experimental.pallas import tpu as pltpu
from jax.sharding import PartitionSpec as P

CH = 32
OUTC = 64
LANES = 128
PX = LANES // CH
F32 = jnp.float32
BF16 = jnp.bfloat16
VMEM = pltpu.VMEM
SMEM = pltpu.SMEM


def up_to(value, step):
    return (value + step - 1) // step * step


def vm():
    return pl.BlockSpec(memory_space=pltpu.VMEM)


def sm():
    return pl.BlockSpec(memory_space=pltpu.SMEM)


def side(axis, toward):
    index = lax.axis_index(axis)
    if toward > 0:
        return index < lax.axis_size(axis) - 1
    return index > 0


def directions(axis):
    return (0,) if lax.axis_size(axis) <= 2 else (1, -1)


def halo_kernel(row_dirs, col_dirs, frames, valid, *refs):
    sends, marks = refs[:-1], refs[-1]
    height = frames.shape[1]
    lanes = frames.shape[2]
    blocks = valid.shape[2]
    last = valid.shape[1] - 1
    wide = lanes // blocks
    for block in range(blocks):
        window = pl.ds(block * wide, wide)
        for spot, line in ((0, last), (3, 0)):
            marks[spot : spot + 1, window] = jnp.full(
                (1, wide), valid[0, line, block].astype(F32), F32
            )
    spots = lax.broadcasted_iota(jnp.int32, (4, lanes), 0)
    tail = frames[0, height - 8 : height, :].astype(F32)[4:8]
    head = frames[0, 0:8, :].astype(F32)[0:4]
    down = jnp.where(spots == 0, marks[0:1, :], tail)
    upper = jnp.where(spots == 3, marks[3:4, :], head)
    bands = {1: down, -1: upper}
    bands[0] = jnp.where(side("row", 1), down, upper)
    columns = {}
    for way, first, block in ((1, lanes - LANES, blocks - 1), (-1, 0, 0)):
        edge = frames[0, :, first : first + LANES].astype(F32)
        flags = jnp.concatenate(
            [
                jnp.full((8, LANES), valid[0, line, block].astype(F32), F32)
                for line in range(last + 1)
            ],
            axis=0,
        )
        columns[way] = jnp.concatenate([edge, flags], axis=0)
    columns[0] = jnp.where(side("col", 1), columns[1], columns[-1])
    outs = iter(sends)
    for way in row_dirs:
        next(outs)[...] = bands[way].astype(BF16)
    for way in col_dirs:
        next(outs)[...] = columns[way].astype(BF16)
    for row_way in row_dirs:
        for col_way in col_dirs:
            right = bands[row_way][:, lanes - LANES :]
            left = bands[row_way][:, :LANES]
            if col_way == 0:
                picked = jnp.where(side("col", 1), right, left)
            else:
                picked = right if col_way > 0 else left
            next(outs)[...] = picked.astype(BF16)


def filter_matrix_kernel(weight, out):
    w = weight[...].astype(F32)
    tiled = jnp.concatenate([w] * PX, axis=1)
    taps = {
        (dy, dx): tiled[(3 * dy + dx) * CH : (3 * dy + dx + 1) * CH]
        for dy in range(3)
        for dx in range(3)
    }
    lane = lax.broadcasted_iota(jnp.int32, (CH, LANES), 1)
    line = lax.broadcasted_iota(jnp.int32, (CH, LANES), 0)
    nothing = jnp.zeros((CH, LANES), F32)
    for q in range(4):
        cell = []
        for v in range(4):
            terms = [
                taps[q - a, v - b]
                for a in range(2)
                for b in range(2)
                if 0 <= q - a < 3 and 0 <= v - b < 3
            ]
            cell.append(functools.reduce(jnp.add, terms) * 0.25)
        for u in range(-1, 2 * PX + 1):
            filt = nothing
            for p in range(PX):
                if 0 <= u - 2 * p + 1 < 4:
                    filt = jnp.where(lane // CH == p, cell[u - 2 * p + 1], filt)
            mean = nothing
            if 0 <= u < 2 * PX and q in (1, 2):
                mean = jnp.where(lane == u // 2 * CH + line, 0.25, nothing)
            spot = {-1: 2 * LANES + LANES - CH, 2 * PX: 2 * LANES}.get(u, u * CH)
            spot += q * 3 * LANES
            out[spot : spot + CH, :LANES] = filt.astype(BF16)
            out[spot : spot + CH, LANES:] = mean.astype(BF16)
        spot = q * 3 * LANES + 2 * LANES + CH
        out[spot : spot + LANES - 2 * CH, :] = jnp.zeros((LANES - 2 * CH, 2 * LANES), BF16)


def encoder_matrix_kernel(weight, out):
    w = weight[...].astype(F32)
    double = jnp.concatenate([w, w], axis=1)
    lane = lax.broadcasted_iota(jnp.int32, (CH, LANES), 1)
    nothing = jnp.zeros((CH, LANES), F32)
    wide = PX * OUTC
    for lag in range(3):
        for dy in range(3):
            base = (lag * 9 + dy * 3) * CH

            def tap(dx):
                if 0 <= dx < 3:
                    return double[base + dx * CH : base + (dx + 1) * CH]
                return nothing

            for u in range(-1, PX + 1):
                spot = {-1: 2 * LANES - CH, PX: LANES}.get(u, u * CH) + dy * 2 * LANES
                for half in range(PX // 2):
                    value = jnp.where(
                        lane < OUTC, tap(u - 2 * half + 1), tap(u - 2 * half)
                    )
                    first = lag * wide + half * LANES
                    out[spot : spot + CH, first : first + LANES] = value.astype(BF16)
            spot = dy * 2 * LANES + LANES + CH
            out[spot : spot + LANES - 2 * CH, lag * wide : (lag + 1) * wide] = jnp.zeros(
                (LANES - 2 * CH, wide), BF16
            )


def pool_kernel(
    order, stride, frames, valid, up, dn, rt, lf, ur, ul, dr, dl, matrix, bias, *refs
):
    outs, (x, pooled) = refs[:-2], refs[-2:]
    height = frames.shape[1]
    lanes = frames.shape[2]
    blocks = valid.shape[2]
    groups = lanes // LANES
    cells = groups // 2 + 1
    rows = height // 2
    held = pooled.shape[0] // outs[0].shape[1]
    has_up = side("row", -1).astype(F32)
    has_dn = side("row", 1).astype(F32)
    has_rt = side("col", 1).astype(F32)
    has_lf = side("col", -1).astype(F32)
    around = groups + 2
    pitch = x.shape[0] // around
    below = 8 + height
    blank = jnp.zeros((pitch - below, LANES), F32)
    right = rt[...].astype(F32) * has_rt
    left = lf[...].astype(F32) * has_lf
    for g in range(around):
        base = g * pitch
        window = pl.ds(g * LANES, LANES)
        if g < groups:
            own = frames[0, :, window].astype(F32)
            over = up[:, window].astype(F32) * has_up
            under = dn[:, window].astype(F32) * has_dn
        elif g == groups:
            own = right[:height]
            over = ur[...].astype(F32) * (has_up * has_rt)
            under = dr[...].astype(F32) * (has_dn * has_rt)
        else:
            own = left[:height]
            over = ul[...].astype(F32) * (has_up * has_lf)
            under = dl[...].astype(F32) * (has_dn * has_lf)
        x[base : base + 4, :] = jnp.zeros((4, LANES), F32)
        x[base + 4 : base + 8, :] = over
        x[base + 8 : base + below, :] = own
        x[base + below : base + pitch, :] = blank
        x[base + below : base + below + 4, :] = under

    lane = lax.broadcasted_iota(jnp.int32, (held, LANES), 1)
    spot = lax.broadcasted_iota(jnp.int32, (held, LANES), 0)
    pieces = []
    for q in range(4):
        strips = [
            x[pl.ds(g * pitch + 5 + q, held, stride=2), :] for g in range(around)
        ]
        pieces.append(jnp.concatenate([strips[2 * c] for c in range(cells)], axis=0))
        pieces.append(jnp.concatenate([strips[2 * c + 1] for c in range(cells)], axis=0))
        pieces.append(
            jnp.concatenate(
                [
                    jnp.where(
                        lane < LANES // 2,
                        strips[(2 * c + 2) % around],
                        strips[(2 * c - 1) % around],
                    )
                    for c in range(cells)
                ],
                axis=0,
            )
        )
    patches = jnp.concatenate([piece.astype(BF16) for piece in pieces], axis=1)
    result = jnp.dot(patches, matrix[...], preferred_element_type=F32)
    shift = jnp.concatenate([bias[...]] * PX, axis=1)
    for c in range(cells):
        if c < blocks:
            base = 2 * c * pitch
            above = x[base + 4 : base + 5, :]
            under = x[base + below + 3 : base + below + 4, :]
            inside = [valid[0, line, c].astype(F32) for line in range(valid.shape[1])]
        else:
            one = lax.broadcasted_iota(jnp.int32, (1, LANES), 1) < LANES // 2

            def both(line):
                first = groups * pitch + line
                second = first + pitch
                return jnp.where(one, x[first : first + 1, :], x[second : second + 1, :])

            above, under = both(4), both(below + 3)
            inside = [
                jnp.where(
                    one,
                    right[height + 8 * line : height + 8 * line + 1],
                    left[height + 8 * line : height + 8 * line + 1],
                )
                for line in range(valid.shape[1])
            ]
        mask = jnp.where(spot == 0, above, jnp.zeros((held, LANES), F32))
        mask = jnp.where(spot == rows + 1, under, mask)
        for line, value in enumerate(inside):
            mask = jnp.where((spot >= 1 + 4 * line) & (spot < 5 + 4 * line), value, mask)
        part = result[c * held : (c + 1) * held]
        pooled[c * held : (c + 1) * held, :] = part[:, LANES:] + mask * (part[:, :LANES] + shift)
    me = lax.axis_index("tm")
    for out, step in zip(outs, order):
        band = step(me)
        for dy in range(stride + 2):
            out[dy] = pooled[pl.ds(band * stride + dy, out.shape[1], stride=held), :].astype(BF16)


def encode_kernel(sources, owner, matrix, bias, *refs):
    count = len(sources)
    arrived = refs[:count]
    out, chunks, folded = refs[count:]
    frames = chunks.shape[0]
    me = lax.axis_index("tm")
    for piece, source in zip(arrived, sources):
        if source is None:
            for slot in range(frames):
                chunks[owner[slot]] = piece[slot].astype(F32)
        else:
            chunks[owner[source(me)]] = piece[...].astype(F32)
    cells = out.shape[3] // (PX * OUTC)
    stride = out.shape[1]
    held = chunks.shape[2]
    kept = up_to(cells, 8)
    lane = lax.broadcasted_iota(jnp.int32, (kept, LANES), 1)
    wide = PX * OUTC
    shift = jnp.concatenate([bias[...]] * PX, axis=1)
    pitch = folded.shape[1] // kept
    for line in range(stride):
        lines = []
        for dy in range(3):
            now, beside = [], []
            for t in range(frames):
                full = chunks[t, line + dy]
                ahead = pltpu.roll(full, held - 1, 0)
                behind = pltpu.roll(full, 1, 0)
                first = lax.broadcasted_iota(jnp.int32, (held, LANES), 0) == 0
                behind = jnp.where(first, full[cells : cells + 1], behind)
                now.append(full[:kept])
                beside.append(jnp.where(lane < LANES // 2, ahead[:kept], behind[:kept]))
            lines.append(jnp.concatenate(now, axis=0).astype(BF16))
            lines.append(jnp.concatenate(beside, axis=0).astype(BF16))
        patches = jnp.concatenate(lines, axis=1)
        result = jnp.dot(patches, matrix[...], preferred_element_type=F32)
        for j in range(frames - 1):
            total = shift
            for lag in range(3):
                t = max(j + 1 - lag, 0)
                total = total + result[t * kept : (t + 1) * kept, lag * wide : (lag + 1) * wide]
            for half in range(wide // LANES):
                folded[half, pl.ds(j, kept, stride=pitch), :] = total[
                    :, half * LANES : (half + 1) * LANES
                ]
        for g in range(cells):
            for half in range(wide // LANES):
                first = g * wide + half * LANES
                out[0, line, :, first : first + LANES] = folded[
                    half, g * pitch : g * pitch + frames - 1, :
                ].astype(BF16)


def ring(axis, shift):
    count = lax.axis_size(axis)
    return [(i, i + shift) for i in range(count) if 0 <= i + shift < count]


def pairs_of(axis, way):
    count = lax.axis_size(axis)
    if way == 0:
        return [(i, count - 1 - i) for i in range(count)]
    return ring(axis, way)


def call(kernel, outs, specs, scratch, name, work=(0, 0)):
    return pl.pallas_call(
        kernel,
        out_shape=outs,
        in_specs=specs,
        out_specs=jax.tree.map(lambda _: vm(), outs),
        scratch_shapes=scratch,
        name=name,
        cost_estimate=pl.CostEstimate(flops=work[0], bytes_accessed=work[1], transcendentals=0),
    )


def on_device(
    frames, owner_map, valid_blocks, deblock_weight, deblock_bias, encoder_weight, encoder_bias
):
    height = frames.shape[1]
    lanes = frames.shape[2]
    bands = lax.axis_size("tm")
    shaped = jax.ShapeDtypeStruct
    row_dirs, col_dirs = directions("row"), directions("col")
    n_col = lax.axis_size("col")

    band = shaped((4, lanes), BF16)
    column = shaped((2 * height, LANES), BF16)
    corner = shaped((4, LANES), BF16)
    sends = call(
        functools.partial(halo_kernel, row_dirs, col_dirs),
        [band] * len(row_dirs)
        + [column] * len(col_dirs)
        + [corner] * (len(row_dirs) * len(col_dirs)),
        [vm(), sm()],
        [VMEM((8, lanes), F32)],
        "halo",
    )(frames, valid_blocks)
    sends = iter(sends)
    by_row = {w: lax.ppermute(next(sends), "row", pairs_of("row", w)) for w in row_dirs}
    by_col = {w: lax.ppermute(next(sends), "col", pairs_of("col", w)) for w in col_dirs}
    by_both = {}
    for w in row_dirs:
        for v in col_dirs:
            pairs = [
                (a * n_col + c, b * n_col + d)
                for a, b in pairs_of("row", w)
                for c, d in pairs_of("col", v)
            ]
            by_both[w, v] = lax.ppermute(next(sends), ("row", "col"), pairs)

    def pick(table, way):
        return table[way] if way in table else table[0]

    def pick_both(w, v):
        return by_both[w if w in row_dirs else 0, v if v in col_dirs else 0]

    filter_matrix = call(
        filter_matrix_kernel,
        shaped((12 * LANES, 2 * LANES), BF16),
        [vm()],
        [],
        "filter_matrix",
        (1 << 22, 1 << 20),
    )(deblock_weight)
    encoder_matrix = call(
        encoder_matrix_kernel,
        shaped((6 * LANES, 3 * PX * OUTC), BF16),
        [vm()],
        [],
        "encoder_matrix",
        (1 << 22, 1 << 20),
    )(encoder_weight)

    rows = height // 2
    stride = rows // bands
    cells = lanes // LANES // 2 + 1
    held = up_to(rows + 2, 8)
    kept = up_to(cells, 8)
    piece = shaped((stride + 2, kept, LANES), BF16)
    direct = bands <= 4 and bands & (bands - 1) == 0
    if direct:
        order = [functools.partial(lambda k, me: me ^ k, k) for k in range(bands)]
    else:
        order = [functools.partial(lambda k, me: k, k) for k in range(bands)]
    parts = call(
        functools.partial(pool_kernel, order, stride),
        [piece] * bands,
        [vm(), sm()] + [vm()] * 10,
        [
            VMEM(((lanes // LANES + 2) * up_to(8 + 2 * held, 8), LANES), F32),
            VMEM((kept * held, LANES), F32),
        ],
        "pool",
        (1 << 22, 1 << 20),
    )(
        frames,
        valid_blocks,
        pick(by_row, 1),
        pick(by_row, -1),
        pick(by_col, -1),
        pick(by_col, 1),
        pick_both(1, -1),
        pick_both(1, 1),
        pick_both(-1, -1),
        pick_both(-1, 1),
        filter_matrix,
        deblock_bias.reshape(1, CH),
    )
    if direct:
        arrived = [parts[0]] + [
            lax.ppermute(parts[k], "tm", [(i, i ^ k) for i in range(bands)])
            for k in range(bands - 1, 0, -1)
        ]
        sources = [order[0]] + [order[k] for k in range(bands - 1, 0, -1)]
    else:
        arrived = [
            lax.all_to_all(jnp.stack(parts), "tm", split_axis=0, concat_axis=0, tiled=True)
        ]
        sources = [None]
    encoded = call(
        functools.partial(encode_kernel, sources),
        shaped((1, stride, bands - 1, lanes // 2 // CH * OUTC), BF16),
        [sm(), vm(), vm()] + [vm()] * len(arrived),
        [
            VMEM((bands, stride + 2, kept, LANES), F32),
            VMEM((PX * OUTC // LANES, kept * up_to(bands - 1, 8), LANES), F32),
        ],
        "encode",
        (1 << 22, 1 << 20),
    )(owner_map, encoder_matrix, encoder_bias.reshape(1, OUTC), *arrived)
    return encoded.transpose(2, 0, 1, 3)


def solution(mesh):
    return jax.shard_map(
        on_device,
        mesh=mesh,
        in_specs=(
            P(("grp", "tm"), "row", "col"),
            P("grp"),
            P(("grp", "tm"), "row", "col"),
            P(),
            P(),
            P(),
            P(),
        ),
        out_specs=P("grp", "row", "tm", "col"),
        check_vma=False,
    )
```

```python
import functools

import jax
import jax.numpy as jnp
from jax import lax
from jax.experimental import pallas as pl
from jax.experimental.pallas import tpu as pltpu
from jax.sharding import PartitionSpec as P

CH = 32
OUTC = 64
LANES = 128
PX = LANES // CH
F32 = jnp.float32
BF16 = jnp.bfloat16
VMEM = pltpu.VMEM
SMEM = pltpu.SMEM
DMA = pltpu.SemaphoreType.DMA


def up_to(value, step):
    return (value + step - 1) // step * step


def vm():
    return pl.BlockSpec(memory_space=pltpu.VMEM)


def far():
    return pl.BlockSpec(memory_space=pltpu.HBM)


def in_far(array):
    return pltpu.with_memory_space_constraint(array, pltpu.HBM)


def fetch(*pairs):
    *pairs, sems = pairs
    copies = [
        pltpu.make_async_copy(source, target, sems.at[i])
        for i, (source, target) in enumerate(pairs)
    ]
    for copy in copies:
        copy.start()
    return copies


def side(axis, toward):
    index = lax.axis_index(axis)
    if toward > 0:
        return index < lax.axis_size(axis) - 1
    return index > 0


def directions(axis):
    return (0,) if lax.axis_size(axis) <= 2 else (1, -1)


def halo_kernel(row_dirs, col_dirs, frames_far, valid_far, frames, *refs):
    sends, (marks, valid, sems) = refs[:-3], refs[-3:]
    whole, flags = fetch((frames_far, frames), (valid_far, valid), sems)
    flags.wait()
    height = frames.shape[1]
    lanes = frames.shape[2]
    blocks = valid.shape[2]
    last = valid.shape[1] - 1
    wide = lanes // blocks
    for block in range(blocks):
        window = pl.ds(block * wide, wide)
        for spot, line in ((0, last), (3, 0)):
            marks[spot : spot + 1, window] = jnp.full(
                (1, wide), valid[0, line, block].astype(F32), F32
            )
    whole.wait()
    spots = lax.broadcasted_iota(jnp.int32, (4, lanes), 0)
    tail = frames[0, height - 8 : height, :].astype(F32)[4:8]
    head = frames[0, 0:8, :].astype(F32)[0:4]
    down = jnp.where(spots == 0, marks[0:1, :], tail)
    upper = jnp.where(spots == 3, marks[3:4, :], head)
    bands = {1: down, -1: upper}
    bands[0] = jnp.where(side("row", 1), down, upper)
    columns = {}
    for way, first, block in ((1, lanes - LANES, blocks - 1), (-1, 0, 0)):
        edge = frames[0, :, first : first + LANES].astype(F32)
        flags = jnp.concatenate(
            [
                jnp.full((8, LANES), valid[0, line, block].astype(F32), F32)
                for line in range(last + 1)
            ],
            axis=0,
        )
        columns[way] = jnp.concatenate([edge, flags], axis=0)
    columns[0] = jnp.where(side("col", 1), columns[1], columns[-1])
    outs = iter(sends)
    for way in row_dirs:
        next(outs)[...] = bands[way].astype(BF16)
    for way in col_dirs:
        next(outs)[...] = columns[way].astype(BF16)
    for row_way in row_dirs:
        for col_way in col_dirs:
            right = bands[row_way][:, lanes - LANES :]
            left = bands[row_way][:, :LANES]
            if col_way == 0:
                picked = jnp.where(side("col", 1), right, left)
            else:
                picked = right if col_way > 0 else left
            next(outs)[...] = picked.astype(BF16)


def turned(weight, staged):
    count = LANES // weight.shape[0]
    values = weight[...].astype(F32)
    staged[:, : values.shape[1]] = jnp.concatenate([values] * count, axis=0)
    return jnp.concatenate(
        [
            jnp.transpose(staged[:, first : first + LANES])
            for first in range(0, staged.shape[1], LANES)
        ],
        axis=0,
    )


def filter_matrix_kernel(
    held, weight_far, bias_far, valid_far, out, shift, masks, weight, bias, valid, staged, sems
):
    copies = fetch((weight_far, weight), (bias_far, bias), (valid_far, valid), sems)
    for copy in copies:
        copy.wait()
    shift[...] = jnp.broadcast_to(jnp.concatenate([bias[...]] * PX, axis=1), shift.shape)
    spots = lax.broadcasted_iota(jnp.int32, (held, LANES), 0)
    for c in range(valid.shape[2]):
        mask = jnp.zeros((held, LANES), F32)
        for line in range(valid.shape[1]):
            inside = (spots >= 1 + 4 * line) & (spots < 5 + 4 * line)
            mask = jnp.where(inside, valid[0, line, c].astype(F32), mask)
        masks[c * held : (c + 1) * held, :] = mask
    tiled = turned(weight, staged)
    taps = {
        (dy, dx): tiled[(3 * dy + dx) * CH : (3 * dy + dx + 1) * CH]
        for dy in range(3)
        for dx in range(3)
    }
    lane = lax.broadcasted_iota(jnp.int32, (CH, LANES), 1)
    line = lax.broadcasted_iota(jnp.int32, (CH, LANES), 0)
    nothing = jnp.zeros((CH, LANES), F32)
    for q in range(4):
        cell = []
        for v in range(4):
            terms = [
                taps[q - a, v - b]
                for a in range(2)
                for b in range(2)
                if 0 <= q - a < 3 and 0 <= v - b < 3
            ]
            cell.append(functools.reduce(jnp.add, terms) * 0.25)
        for u in range(-1, 2 * PX + 1):
            filt = nothing
            for p in range(PX):
                if 0 <= u - 2 * p + 1 < 4:
                    filt = jnp.where(lane // CH == p, cell[u - 2 * p + 1], filt)
            mean = nothing
            if 0 <= u < 2 * PX and q in (1, 2):
                mean = jnp.where(lane == u // 2 * CH + line, 0.25, nothing)
            spot = {-1: 2 * LANES + LANES - CH, 2 * PX: 2 * LANES}.get(u, u * CH)
            spot += q * 3 * LANES
            out[spot : spot + CH, :LANES] = filt.astype(BF16)
            out[spot : spot + CH, LANES:] = mean.astype(BF16)
        spot = q * 3 * LANES + 2 * LANES + CH
        out[spot : spot + LANES - 2 * CH, :] = jnp.zeros((LANES - 2 * CH, 2 * LANES), BF16)


def encoder_matrix_kernel(
    sources, weight_far, bias_far, owner_far, out, shift, picks, weight, bias, owner, staged, sems
):
    copies = fetch((weight_far, weight), (bias_far, bias), (owner_far, owner), sems)
    for copy in copies:
        copy.wait()
    shift[...] = jnp.broadcast_to(jnp.concatenate([bias[...]] * PX, axis=1), shift.shape)
    me = lax.axis_index("tm")
    for spot, source in enumerate(sources):
        time = jnp.full(picks.shape[1:], owner[source(me)], jnp.int32)
        picks[spot] = time
    double = turned(weight, staged)
    lane = lax.broadcasted_iota(jnp.int32, (CH, LANES), 1)
    nothing = jnp.zeros((CH, LANES), F32)
    wide = PX * OUTC
    for lag in range(3):
        for dy in range(3):
            base = (lag * 9 + dy * 3) * CH

            def tap(dx):
                if 0 <= dx < 3:
                    return double[base + dx * CH : base + (dx + 1) * CH]
                return nothing

            for u in range(-1, PX + 1):
                spot = {-1: 2 * LANES - CH, PX: LANES}.get(u, u * CH) + dy * 2 * LANES
                for half in range(PX // 2):
                    value = jnp.where(
                        lane < OUTC, tap(u - 2 * half + 1), tap(u - 2 * half)
                    )
                    first = lag * wide + half * LANES
                    out[spot : spot + CH, first : first + LANES] = value.astype(BF16)
            spot = dy * 2 * LANES + LANES + CH
            out[spot : spot + LANES - 2 * CH, lag * wide : (lag + 1) * wide] = jnp.zeros(
                (LANES - 2 * CH, wide), BF16
            )


def pool_kernel(
    order, stride, frames, up, dn, rt, lf, ur, ul, dr, dl, matrix, bias, masks, *refs
):
    outs, (x, pooled) = refs[:-2], refs[-2:]
    height = frames.shape[1]
    lanes = frames.shape[2]
    groups = lanes // LANES
    blocks = groups // 2
    cells = groups // 2 + 1
    rows = height // 2
    held = pooled.shape[0] // outs[0].shape[1]
    has_up = side("row", -1).astype(F32)
    has_dn = side("row", 1).astype(F32)
    has_rt = side("col", 1).astype(F32)
    has_lf = side("col", -1).astype(F32)
    around = groups + 2
    pitch = x.shape[0] // around
    below = 8 + height
    blank = jnp.zeros((pitch - below, LANES), F32)
    right = rt[...].astype(F32) * has_rt
    left = lf[...].astype(F32) * has_lf
    for g in range(around):
        base = g * pitch
        window = pl.ds(g * LANES, LANES)
        if g < groups:
            own = frames[0, :, window].astype(F32)
            over = up[:, window].astype(F32) * has_up
            under = dn[:, window].astype(F32) * has_dn
        elif g == groups:
            own = right[:height]
            over = ur[...].astype(F32) * (has_up * has_rt)
            under = dr[...].astype(F32) * (has_dn * has_rt)
        else:
            own = left[:height]
            over = ul[...].astype(F32) * (has_up * has_lf)
            under = dl[...].astype(F32) * (has_dn * has_lf)
        x[base : base + 4, :] = jnp.zeros((4, LANES), F32)
        x[base + 4 : base + 8, :] = over
        x[base + 8 : base + below, :] = own
        x[base + below : base + pitch, :] = blank
        x[base + below : base + below + 4, :] = under

    lane = lax.broadcasted_iota(jnp.int32, (held, LANES), 1)
    spot = lax.broadcasted_iota(jnp.int32, (held, LANES), 0)
    pieces = []
    for q in range(4):
        strips = [
            x[pl.ds(g * pitch + 5 + q, held, stride=2), :] for g in range(around)
        ]
        pieces.append(jnp.concatenate([strips[2 * c] for c in range(cells)], axis=0))
        pieces.append(jnp.concatenate([strips[2 * c + 1] for c in range(cells)], axis=0))
        pieces.append(
            jnp.concatenate(
                [
                    jnp.where(
                        lane < LANES // 2,
                        strips[(2 * c + 2) % around],
                        strips[(2 * c - 1) % around],
                    )
                    for c in range(cells)
                ],
                axis=0,
            )
        )
    patches = jnp.concatenate([piece.astype(BF16) for piece in pieces], axis=1)
    result = jnp.dot(patches, matrix[...], preferred_element_type=F32)
    shift = bias[0:1, :]
    for c in range(cells):
        mask = jnp.zeros((held, LANES), F32)
        if c < blocks:
            base = 2 * c * pitch
            above = x[base + 4 : base + 5, :]
            under = x[base + below + 3 : base + below + 4, :]
            mask = masks[c * held : (c + 1) * held, :]
            inside = []
        else:
            one = lax.broadcasted_iota(jnp.int32, (1, LANES), 1) < LANES // 2

            def both(line):
                first = groups * pitch + line
                second = first + pitch
                return jnp.where(one, x[first : first + 1, :], x[second : second + 1, :])

            above, under = both(4), both(below + 3)
            inside = [
                jnp.where(
                    one,
                    right[height + 8 * line : height + 8 * line + 1],
                    left[height + 8 * line : height + 8 * line + 1],
                )
                for line in range(height // 8)
            ]
        mask = jnp.where(spot == 0, above, mask)
        mask = jnp.where(spot == rows + 1, under, mask)
        for line, value in enumerate(inside):
            mask = jnp.where((spot >= 1 + 4 * line) & (spot < 5 + 4 * line), value, mask)
        part = result[c * held : (c + 1) * held]
        pooled[c * held : (c + 1) * held, :] = part[:, LANES:] + mask * (part[:, :LANES] + shift)
    me = lax.axis_index("tm")
    for out, step in zip(outs, order):
        band = step(me)
        for dy in range(stride + 2):
            out[dy] = pooled[pl.ds(band * stride + dy, out.shape[1], stride=held), :].astype(BF16)


def encode_kernel(matrix, bias, picks, *refs):
    arrived, (out, chunks, folded) = refs[:-3], refs[-3:]
    frames = chunks.shape[0]
    if len(arrived) == frames:
        pieces = [piece[...].astype(F32) for piece in arrived]
    else:
        pieces = [arrived[0][slot].astype(F32) for slot in range(frames)]
    lines = pieces[0].shape[0]
    for t in range(frames):
        for dy in range(lines):
            chosen = pieces[0][dy]
            for slot in range(1, frames):
                chosen = jnp.where(picks[slot] == t, pieces[slot][dy], chosen)
            chunks[t, dy] = chosen
    cells = out.shape[3] // (PX * OUTC)
    stride = out.shape[1]
    held = chunks.shape[2]
    kept = up_to(cells, 8)
    lane = lax.broadcasted_iota(jnp.int32, (kept, LANES), 1)
    wide = PX * OUTC
    shift = bias[0:1, :]
    pitch = folded.shape[1] // kept
    for line in range(stride):
        lines = []
        for dy in range(3):
            now, beside = [], []
            for t in range(frames):
                full = chunks[t, line + dy]
                ahead = pltpu.roll(full, held - 1, 0)
                behind = pltpu.roll(full, 1, 0)
                first = lax.broadcasted_iota(jnp.int32, (held, LANES), 0) == 0
                behind = jnp.where(first, full[cells : cells + 1], behind)
                now.append(full[:kept])
                beside.append(jnp.where(lane < LANES // 2, ahead[:kept], behind[:kept]))
            lines.append(jnp.concatenate(now, axis=0).astype(BF16))
            lines.append(jnp.concatenate(beside, axis=0).astype(BF16))
        patches = jnp.concatenate(lines, axis=1)
        result = jnp.dot(patches, matrix[...], preferred_element_type=F32)
        for j in range(frames - 1):
            total = shift
            for lag in range(3):
                t = max(j + 1 - lag, 0)
                total = total + result[t * kept : (t + 1) * kept, lag * wide : (lag + 1) * wide]
            for half in range(wide // LANES):
                folded[half, pl.ds(j, kept, stride=pitch), :] = total[
                    :, half * LANES : (half + 1) * LANES
                ]
        for g in range(cells):
            for half in range(wide // LANES):
                first = g * wide + half * LANES
                out[0, line, :, first : first + LANES] = folded[
                    half, g * pitch : g * pitch + frames - 1, :
                ].astype(BF16)


def ring(axis, shift):
    count = lax.axis_size(axis)
    return [(i, i + shift) for i in range(count) if 0 <= i + shift < count]


def pairs_of(axis, way):
    count = lax.axis_size(axis)
    if way == 0:
        return [(i, count - 1 - i) for i in range(count)]
    return ring(axis, way)


def call(kernel, outs, specs, scratch, name, work=(0, 0), limit=16):
    return pl.pallas_call(
        kernel,
        out_shape=outs,
        in_specs=specs,
        out_specs=jax.tree.map(lambda _: vm(), outs),
        scratch_shapes=scratch,
        name=name,
        compiler_params=pltpu.CompilerParams(vmem_limit_bytes=limit << 20),
        cost_estimate=pl.CostEstimate(flops=work[0], bytes_accessed=work[1], transcendentals=0),
    )


def on_device(
    frames, owner_map, valid_blocks, deblock_weight, deblock_bias, encoder_weight, encoder_bias
):
    height = frames.shape[1]
    lanes = frames.shape[2]
    bands = lax.axis_size("tm")
    shaped = jax.ShapeDtypeStruct
    row_dirs, col_dirs = directions("row"), directions("col")
    n_col = lax.axis_size("col")

    band = shaped((4, lanes), BF16)
    column = shaped((2 * height, LANES), BF16)
    corner = shaped((4, LANES), BF16)
    own, *sends = call(
        functools.partial(halo_kernel, row_dirs, col_dirs),
        [shaped(frames.shape, BF16)]
        + [band] * len(row_dirs)
        + [column] * len(col_dirs)
        + [corner] * (len(row_dirs) * len(col_dirs)),
        [far(), far()],
        [VMEM((8, lanes), F32), SMEM(valid_blocks.shape, jnp.int32), DMA((2,))],
        "halo",
    )(in_far(frames), in_far(valid_blocks))
    sends = iter(sends)
    by_row = {w: lax.ppermute(next(sends), "row", pairs_of("row", w)) for w in row_dirs}
    by_col = {w: lax.ppermute(next(sends), "col", pairs_of("col", w)) for w in col_dirs}
    by_both = {}
    for w in row_dirs:
        for v in col_dirs:
            pairs = [
                (a * n_col + c, b * n_col + d)
                for a, b in pairs_of("row", w)
                for c, d in pairs_of("col", v)
            ]
            by_both[w, v] = lax.ppermute(next(sends), ("row", "col"), pairs)

    def pick(table, way):
        return table[way] if way in table else table[0]

    def pick_both(w, v):
        return by_both[w if w in row_dirs else 0, v if v in col_dirs else 0]

    rows = height // 2
    stride = rows // bands
    cells = lanes // LANES // 2 + 1
    held = up_to(rows + 2, 8)
    kept = up_to(cells, 8)
    piece = shaped((stride + 2, kept, LANES), BF16)
    filter_matrix, filter_shift, masks = call(
        functools.partial(filter_matrix_kernel, held),
        [
            shaped((12 * LANES, 2 * LANES), BF16),
            shaped((8, LANES), F32),
            shaped(((cells - 1) * held, LANES), F32),
        ],
        [far()] * 3,
        [
            VMEM((CH, 9 * CH), BF16),
            VMEM((1, CH), F32),
            SMEM(valid_blocks.shape, jnp.int32),
            VMEM((LANES, up_to(9 * CH, LANES)), F32),
            DMA((3,)),
        ],
        "filter_matrix",
        (1 << 22, 1 << 20),
    )(in_far(deblock_weight.T), in_far(deblock_bias.reshape(1, CH)), in_far(valid_blocks))
    direct = bands <= 4 and bands & (bands - 1) == 0
    if direct:
        order = [functools.partial(lambda k, me: me ^ k, k) for k in range(bands)]
    else:
        order = [functools.partial(lambda k, me: k, k) for k in range(bands)]
    parts = call(
        functools.partial(pool_kernel, order, stride),
        [piece] * bands,
        [vm()] * 12,
        [
            VMEM(((lanes // LANES + 2) * up_to(8 + 2 * held, 8), LANES), F32),
            VMEM((kept * held, LANES), F32),
        ],
        "pool",
        (1 << 22, 1 << 20),
    )(
        own,
        pick(by_row, 1),
        pick(by_row, -1),
        pick(by_col, -1),
        pick(by_col, 1),
        pick_both(1, -1),
        pick_both(1, 1),
        pick_both(-1, -1),
        pick_both(-1, 1),
        filter_matrix,
        filter_shift,
        masks,
    )
    if direct:
        arrived = [parts[0]] + [
            lax.ppermute(parts[k], "tm", [(i, i ^ k) for i in range(bands)])
            for k in range(1, bands)
        ]
    else:
        arrived = [
            lax.all_to_all(jnp.stack(parts), "tm", split_axis=0, concat_axis=0, tiled=True)
        ]
    encoder_matrix, encoder_shift, picks = call(
        functools.partial(encoder_matrix_kernel, order),
        [
            shaped((6 * LANES, 3 * PX * OUTC), BF16),
            shaped((8, PX * OUTC), F32),
            shaped((bands, kept, LANES), jnp.int32),
        ],
        [far()] * 3,
        [
            VMEM((OUTC, 27 * CH), BF16),
            VMEM((1, OUTC), F32),
            SMEM(owner_map.shape, jnp.int32),
            VMEM((LANES, up_to(27 * CH, LANES)), F32),
            DMA((3,)),
        ],
        "encoder_matrix",
        (1 << 22, 1 << 20),
    )(in_far(encoder_weight.T), in_far(encoder_bias.reshape(1, OUTC)), in_far(owner_map))
    encoded = call(
        encode_kernel,
        shaped((1, stride, bands - 1, lanes // 2 // CH * OUTC), BF16),
        [vm()] * (3 + len(arrived)),
        [
            VMEM((bands, stride + 2, kept, LANES), F32),
            VMEM((PX * OUTC // LANES, kept * up_to(bands - 1, 8), LANES), F32),
        ],
        "encode",
        (1 << 22, 1 << 20),
    )(encoder_matrix, encoder_shift, picks, *arrived)
    return encoded.transpose(2, 0, 1, 3)


def solution(mesh):
    return jax.shard_map(
        on_device,
        mesh=mesh,
        in_specs=(
            P(("grp", "tm"), "row", "col"),
            P("grp"),
            P(("grp", "tm"), "row", "col"),
            P(),
            P(),
            P(),
            P(),
        ),
        out_specs=P("grp", "row", "tm", "col"),
        check_vma=False,
    )
```

```python
import functools

import jax
import jax.numpy as jnp
from jax import lax
from jax.experimental import pallas as pl
from jax.experimental.pallas import tpu as pltpu
from jax.sharding import PartitionSpec as P

CH = 32
OUTC = 64
LANES = 128
PX = LANES // CH
F32 = jnp.float32
BF16 = jnp.bfloat16
VMEM = pltpu.VMEM
SMEM = pltpu.SMEM
DMA = pltpu.SemaphoreType.DMA


def up_to(value, step):
    return (value + step - 1) // step * step


def vm():
    return pl.BlockSpec(memory_space=pltpu.VMEM)


def far():
    return pl.BlockSpec(memory_space=pltpu.HBM)


def in_far(array):
    return pltpu.with_memory_space_constraint(array, pltpu.HBM)


def fetch(*pairs):
    *pairs, sems = pairs
    copies = [
        pltpu.make_async_copy(source, target, sems.at[i])
        for i, (source, target) in enumerate(pairs)
    ]
    for copy in copies:
        copy.start()
    return copies


def side(axis, toward):
    index = lax.axis_index(axis)
    if toward > 0:
        return index < lax.axis_size(axis) - 1
    return index > 0


def directions(axis):
    return (0,) if lax.axis_size(axis) <= 2 else (1, -1)


def halo_kernel(row_dirs, col_dirs, frames_far, valid_far, frames, *refs):
    sends, (marks, valid, sems) = refs[:-3], refs[-3:]
    whole, flags = fetch((frames_far, frames), (valid_far, valid), sems)
    flags.wait()
    height = frames.shape[1]
    lanes = frames.shape[2]
    blocks = valid.shape[2]
    last = valid.shape[1] - 1
    wide = lanes // blocks
    for block in range(blocks):
        window = pl.ds(block * wide, wide)
        for spot, line in ((0, last), (3, 0)):
            marks[spot : spot + 1, window] = jnp.full(
                (1, wide), valid[0, line, block].astype(F32), F32
            )
    whole.wait()
    spots = lax.broadcasted_iota(jnp.int32, (4, lanes), 0)
    tail = frames[0, height - 8 : height, :].astype(F32)[4:8]
    head = frames[0, 0:8, :].astype(F32)[0:4]
    down = jnp.where(spots == 0, marks[0:1, :], tail)
    upper = jnp.where(spots == 3, marks[3:4, :], head)
    bands = {1: down, -1: upper}
    bands[0] = jnp.where(side("row", 1), down, upper)
    columns = {}
    for way, first, block in ((1, lanes - LANES, blocks - 1), (-1, 0, 0)):
        edge = frames[0, :, first : first + LANES].astype(F32)
        flags = jnp.concatenate(
            [
                jnp.full((8, LANES), valid[0, line, block].astype(F32), F32)
                for line in range(last + 1)
            ],
            axis=0,
        )
        columns[way] = jnp.concatenate([edge, flags], axis=0)
    columns[0] = jnp.where(side("col", 1), columns[1], columns[-1])
    outs = iter(sends)
    for way in row_dirs:
        next(outs)[...] = bands[way].astype(BF16)
    for way in col_dirs:
        next(outs)[...] = columns[way].astype(BF16)
    for row_way in row_dirs:
        for col_way in col_dirs:
            right = bands[row_way][:, lanes - LANES :]
            left = bands[row_way][:, :LANES]
            if col_way == 0:
                picked = jnp.where(side("col", 1), right, left)
            else:
                picked = right if col_way > 0 else left
            next(outs)[...] = picked.astype(BF16)


def turned(weight, staged):
    count = LANES // weight.shape[0]
    values = weight[...].astype(F32)
    staged[:, : values.shape[1]] = jnp.concatenate([values] * count, axis=0)
    return jnp.concatenate(
        [
            jnp.transpose(staged[:, first : first + LANES])
            for first in range(0, staged.shape[1], LANES)
        ],
        axis=0,
    )


def prepare_kernel(held, sources, *refs):
    far_refs, refs = refs[:6], refs[6:]
    filter_outs, encoder_outs, refs = refs[:3], refs[3:6], refs[6:]
    near_refs, (filter_staged, encoder_staged, sems) = refs[:6], refs[6:]
    copies = fetch(*zip(far_refs, near_refs), sems)
    for copy in copies:
        copy.wait()
    filter_matrix(held, *filter_outs, *near_refs[:3], filter_staged)
    encoder_matrix(sources, *encoder_outs, *near_refs[3:], encoder_staged)


def filter_matrix(held, out, shift, masks, weight, bias, valid, staged):
    shift[...] = jnp.broadcast_to(jnp.concatenate([bias[...]] * PX, axis=1), shift.shape)
    spots = lax.broadcasted_iota(jnp.int32, (held, LANES), 0)
    for c in range(valid.shape[2]):
        mask = jnp.zeros((held, LANES), F32)
        for line in range(valid.shape[1]):
            inside = (spots >= 1 + 4 * line) & (spots < 5 + 4 * line)
            mask = jnp.where(inside, valid[0, line, c].astype(F32), mask)
        masks[c * held : (c + 1) * held, :] = mask
    tiled = turned(weight, staged)
    taps = {
        (dy, dx): tiled[(3 * dy + dx) * CH : (3 * dy + dx + 1) * CH]
        for dy in range(3)
        for dx in range(3)
    }
    lane = lax.broadcasted_iota(jnp.int32, (CH, LANES), 1)
    line = lax.broadcasted_iota(jnp.int32, (CH, LANES), 0)
    nothing = jnp.zeros((CH, LANES), F32)
    for q in range(4):
        cell = []
        for v in range(4):
            terms = [
                taps[q - a, v - b]
                for a in range(2)
                for b in range(2)
                if 0 <= q - a < 3 and 0 <= v - b < 3
            ]
            cell.append(functools.reduce(jnp.add, terms) * 0.25)
        for u in range(-1, 2 * PX + 1):
            filt = nothing
            for p in range(PX):
                if 0 <= u - 2 * p + 1 < 4:
                    filt = jnp.where(lane // CH == p, cell[u - 2 * p + 1], filt)
            mean = nothing
            if 0 <= u < 2 * PX and q in (1, 2):
                mean = jnp.where(lane == u // 2 * CH + line, 0.25, nothing)
            spot = {-1: 2 * LANES + LANES - CH, 2 * PX: 2 * LANES}.get(u, u * CH)
            spot += q * 3 * LANES
            out[spot : spot + CH, :LANES] = filt.astype(BF16)
            out[spot : spot + CH, LANES:] = mean.astype(BF16)
        spot = q * 3 * LANES + 2 * LANES + CH
        out[spot : spot + LANES - 2 * CH, :] = jnp.zeros((LANES - 2 * CH, 2 * LANES), BF16)


def encoder_matrix(sources, out, shift, picks, weight, bias, owner, staged):
    shift[...] = jnp.broadcast_to(jnp.concatenate([bias[...]] * PX, axis=1), shift.shape)
    me = lax.axis_index("tm")
    for spot, source in enumerate(sources):
        time = jnp.full(picks.shape[1:], owner[source(me)], jnp.int32)
        picks[spot] = time
    double = turned(weight, staged)
    lane = lax.broadcasted_iota(jnp.int32, (CH, LANES), 1)
    nothing = jnp.zeros((CH, LANES), F32)
    wide = PX * OUTC
    for lag in range(3):
        for dy in range(3):
            base = (lag * 9 + dy * 3) * CH

            def tap(dx):
                if 0 <= dx < 3:
                    return double[base + dx * CH : base + (dx + 1) * CH]
                return nothing

            for u in range(-1, PX + 1):
                spot = {-1: 2 * LANES - CH, PX: LANES}.get(u, u * CH) + dy * 2 * LANES
                for half in range(PX // 2):
                    value = jnp.where(
                        lane < OUTC, tap(u - 2 * half + 1), tap(u - 2 * half)
                    )
                    first = lag * wide + half * LANES
                    out[spot : spot + CH, first : first + LANES] = value.astype(BF16)
            spot = dy * 2 * LANES + LANES + CH
            out[spot : spot + LANES - 2 * CH, lag * wide : (lag + 1) * wide] = jnp.zeros(
                (LANES - 2 * CH, wide), BF16
            )


def pool_kernel(
    order, stride, frames, up, dn, rt, lf, ur, ul, dr, dl, matrix, bias, masks, *refs
):
    outs, (x, pooled) = refs[:-2], refs[-2:]
    height = frames.shape[1]
    lanes = frames.shape[2]
    groups = lanes // LANES
    blocks = groups // 2
    cells = groups // 2 + 1
    rows = height // 2
    held = pooled.shape[0] // outs[0].shape[1]
    has_up = side("row", -1).astype(F32)
    has_dn = side("row", 1).astype(F32)
    has_rt = side("col", 1).astype(F32)
    has_lf = side("col", -1).astype(F32)
    around = groups + 2
    pitch = x.shape[0] // around
    below = 8 + height
    blank = jnp.zeros((pitch - below, LANES), F32)
    right = rt[...].astype(F32) * has_rt
    left = lf[...].astype(F32) * has_lf
    for g in range(around):
        base = g * pitch
        window = pl.ds(g * LANES, LANES)
        if g < groups:
            own = frames[0, :, window].astype(F32)
            over = up[:, window].astype(F32) * has_up
            under = dn[:, window].astype(F32) * has_dn
        elif g == groups:
            own = right[:height]
            over = ur[...].astype(F32) * (has_up * has_rt)
            under = dr[...].astype(F32) * (has_dn * has_rt)
        else:
            own = left[:height]
            over = ul[...].astype(F32) * (has_up * has_lf)
            under = dl[...].astype(F32) * (has_dn * has_lf)
        x[base : base + 4, :] = jnp.zeros((4, LANES), F32)
        x[base + 4 : base + 8, :] = over
        x[base + 8 : base + below, :] = own
        x[base + below : base + pitch, :] = blank
        x[base + below : base + below + 4, :] = under

    lane = lax.broadcasted_iota(jnp.int32, (held, LANES), 1)
    spot = lax.broadcasted_iota(jnp.int32, (held, LANES), 0)
    pieces = []
    for q in range(4):
        strips = [
            x[pl.ds(g * pitch + 5 + q, held, stride=2), :] for g in range(around)
        ]
        pieces.append(jnp.concatenate([strips[2 * c] for c in range(cells)], axis=0))
        pieces.append(jnp.concatenate([strips[2 * c + 1] for c in range(cells)], axis=0))
        pieces.append(
            jnp.concatenate(
                [
                    jnp.where(
                        lane < LANES // 2,
                        strips[(2 * c + 2) % around],
                        strips[(2 * c - 1) % around],
                    )
                    for c in range(cells)
                ],
                axis=0,
            )
        )
    patches = jnp.concatenate([piece.astype(BF16) for piece in pieces], axis=1)
    result = jnp.dot(patches, matrix[...], preferred_element_type=F32)
    shift = bias[0:1, :]
    for c in range(cells):
        mask = jnp.zeros((held, LANES), F32)
        if c < blocks:
            base = 2 * c * pitch
            above = x[base + 4 : base + 5, :]
            under = x[base + below + 3 : base + below + 4, :]
            mask = masks[c * held : (c + 1) * held, :]
            inside = []
        else:
            one = lax.broadcasted_iota(jnp.int32, (1, LANES), 1) < LANES // 2

            def both(line):
                first = groups * pitch + line
                second = first + pitch
                return jnp.where(one, x[first : first + 1, :], x[second : second + 1, :])

            above, under = both(4), both(below + 3)
            inside = [
                jnp.where(
                    one,
                    right[height + 8 * line : height + 8 * line + 1],
                    left[height + 8 * line : height + 8 * line + 1],
                )
                for line in range(height // 8)
            ]
        mask = jnp.where(spot == 0, above, mask)
        mask = jnp.where(spot == rows + 1, under, mask)
        for line, value in enumerate(inside):
            mask = jnp.where((spot >= 1 + 4 * line) & (spot < 5 + 4 * line), value, mask)
        part = result[c * held : (c + 1) * held]
        pooled[c * held : (c + 1) * held, :] = part[:, LANES:] + mask * (part[:, :LANES] + shift)
    me = lax.axis_index("tm")
    for out, step in zip(outs, order):
        band = step(me)
        for dy in range(stride + 2):
            out[dy] = pooled[pl.ds(band * stride + dy, out.shape[1], stride=held), :].astype(BF16)


def encode_kernel(matrix, bias, picks, *refs):
    arrived, (out, chunks, folded) = refs[:-3], refs[-3:]
    frames = chunks.shape[0]
    if len(arrived) == frames:
        pieces = [piece[...].astype(F32) for piece in arrived]
    else:
        pieces = [arrived[0][slot].astype(F32) for slot in range(frames)]
    lines = pieces[0].shape[0]
    for t in range(frames):
        for dy in range(lines):
            chosen = pieces[0][dy]
            for slot in range(1, frames):
                chosen = jnp.where(picks[slot] == t, pieces[slot][dy], chosen)
            chunks[t, dy] = chosen
    cells = out.shape[3] // (PX * OUTC)
    stride = out.shape[1]
    held = chunks.shape[2]
    kept = up_to(cells, 8)
    lane = lax.broadcasted_iota(jnp.int32, (kept, LANES), 1)
    wide = PX * OUTC
    shift = bias[0:1, :]
    pitch = folded.shape[1] // kept
    for line in range(stride):
        lines = []
        for dy in range(3):
            now, beside = [], []
            for t in range(frames):
                full = chunks[t, line + dy]
                ahead = pltpu.roll(full, held - 1, 0)
                behind = pltpu.roll(full, 1, 0)
                first = lax.broadcasted_iota(jnp.int32, (held, LANES), 0) == 0
                behind = jnp.where(first, full[cells : cells + 1], behind)
                now.append(full[:kept])
                beside.append(jnp.where(lane < LANES // 2, ahead[:kept], behind[:kept]))
            lines.append(jnp.concatenate(now, axis=0).astype(BF16))
            lines.append(jnp.concatenate(beside, axis=0).astype(BF16))
        patches = jnp.concatenate(lines, axis=1)
        result = jnp.dot(patches, matrix[...], preferred_element_type=F32)
        for j in range(frames - 1):
            total = shift
            for lag in range(3):
                t = max(j + 1 - lag, 0)
                total = total + result[t * kept : (t + 1) * kept, lag * wide : (lag + 1) * wide]
            for half in range(wide // LANES):
                folded[half, pl.ds(j, kept, stride=pitch), :] = total[
                    :, half * LANES : (half + 1) * LANES
                ]
        for g in range(cells):
            for half in range(wide // LANES):
                first = g * wide + half * LANES
                out[0, line, :, first : first + LANES] = folded[
                    half, g * pitch : g * pitch + frames - 1, :
                ].astype(BF16)


def ring(axis, shift):
    count = lax.axis_size(axis)
    return [(i, i + shift) for i in range(count) if 0 <= i + shift < count]


def pairs_of(axis, way):
    count = lax.axis_size(axis)
    if way == 0:
        return [(i, count - 1 - i) for i in range(count)]
    return ring(axis, way)


def call(kernel, outs, specs, scratch, work=(0, 0), limit=16):
    return pl.pallas_call(
        kernel,
        out_shape=outs,
        in_specs=specs,
        out_specs=jax.tree.map(lambda _: vm(), outs),
        scratch_shapes=scratch,
        compiler_params=pltpu.CompilerParams(vmem_limit_bytes=limit << 20),
        cost_estimate=pl.CostEstimate(flops=work[0], bytes_accessed=work[1], transcendentals=0),
    )


def on_device(
    frames, owner_map, valid_blocks, deblock_weight, deblock_bias, encoder_weight, encoder_bias
):
    height = frames.shape[1]
    lanes = frames.shape[2]
    bands = lax.axis_size("tm")
    shaped = jax.ShapeDtypeStruct
    row_dirs, col_dirs = directions("row"), directions("col")
    n_col = lax.axis_size("col")

    band = shaped((4, lanes), BF16)
    column = shaped((2 * height, LANES), BF16)
    corner = shaped((4, LANES), BF16)
    own, *sends = call(
        functools.partial(halo_kernel, row_dirs, col_dirs),
        [shaped(frames.shape, BF16)]
        + [band] * len(row_dirs)
        + [column] * len(col_dirs)
        + [corner] * (len(row_dirs) * len(col_dirs)),
        [far(), far()],
        [VMEM((8, lanes), F32), SMEM(valid_blocks.shape, jnp.int32), DMA((2,))],
    )(in_far(frames), in_far(valid_blocks))
    sends = iter(sends)
    by_row, by_col = {}, {}
    for w in row_dirs:
        by_row[w] = lax.ppermute(next(sends), "row", pairs_of("row", w))
    for w in col_dirs:
        by_col[w] = lax.ppermute(next(sends), "col", pairs_of("col", w))
    by_both = {}
    for w in row_dirs:
        for v in col_dirs:
            pairs = [
                (a * n_col + c, b * n_col + d)
                for a, b in pairs_of("row", w)
                for c, d in pairs_of("col", v)
            ]
            by_both[w, v] = lax.ppermute(next(sends), ("row", "col"), pairs)

    def pick(table, way):
        return table[way] if way in table else table[0]

    def pick_both(w, v):
        return by_both[w if w in row_dirs else 0, v if v in col_dirs else 0]

    rows = height // 2
    stride = rows // bands
    cells = lanes // LANES // 2 + 1
    held = up_to(rows + 2, 8)
    kept = up_to(cells, 8)
    piece = shaped((stride + 2, kept, LANES), BF16)
    direct = bands <= 4
    if direct:
        order = [functools.partial(lambda k, me: lax.rem(me + k, bands), k) for k in range(bands)]
        sources = [
            functools.partial(lambda k, me: lax.rem(me + bands - k, bands), k)
            for k in range(bands)
        ]
    else:
        order = [functools.partial(lambda k, me: k, k) for k in range(bands)]
        sources = order
    filter_table, filter_shift, masks, encoder_table, encoder_shift, picks = call(
        functools.partial(prepare_kernel, held, sources),
        [
            shaped((12 * LANES, 2 * LANES), BF16),
            shaped((8, LANES), F32),
            shaped(((cells - 1) * held, LANES), F32),
            shaped((6 * LANES, 3 * PX * OUTC), BF16),
            shaped((8, PX * OUTC), F32),
            shaped((bands, kept, LANES), jnp.int32),
        ],
        [far()] * 6,
        [
            VMEM((CH, 9 * CH), BF16),
            VMEM((1, CH), F32),
            SMEM(valid_blocks.shape, jnp.int32),
            VMEM((OUTC, 27 * CH), BF16),
            VMEM((1, OUTC), F32),
            SMEM(owner_map.shape, jnp.int32),
            VMEM((LANES, up_to(9 * CH, LANES)), F32),
            VMEM((LANES, up_to(27 * CH, LANES)), F32),
            DMA((6,)),
        ],
        (1 << 22, 1 << 20),
    )(
        in_far(deblock_weight.T),
        in_far(deblock_bias.reshape(1, CH)),
        in_far(valid_blocks),
        in_far(encoder_weight.T),
        in_far(encoder_bias.reshape(1, OUTC)),
        in_far(owner_map),
    )
    parts = call(
        functools.partial(pool_kernel, order, stride),
        [piece] * bands,
        [vm()] * 12,
        [
            VMEM(((lanes // LANES + 2) * up_to(8 + 2 * held, 8), LANES), F32),
            VMEM((kept * held, LANES), F32),
        ],
        (1 << 22, 1 << 20),
    )(
        own,
        pick(by_row, 1),
        pick(by_row, -1),
        pick(by_col, -1),
        pick(by_col, 1),
        pick_both(1, -1),
        pick_both(1, 1),
        pick_both(-1, -1),
        pick_both(-1, 1),
        filter_table,
        filter_shift,
        masks,
    )
    if direct:
        arrived = [parts[0]]
        for k in range(1, bands):
            pairs = [(i, (i + k) % bands) for i in range(bands)]
            arrived.append(lax.ppermute(parts[k], "tm", pairs))
    else:
        arrived = [
            lax.all_to_all(jnp.stack(parts), "tm", split_axis=0, concat_axis=0, tiled=True)
        ]
    encoded = call(
        encode_kernel,
        shaped((1, stride, bands - 1, lanes // 2 // CH * OUTC), BF16),
        [vm()] * (3 + len(arrived)),
        [
            VMEM((bands, stride + 2, kept, LANES), F32),
            VMEM((PX * OUTC // LANES, kept * up_to(bands - 1, 8), LANES), F32),
        ],
        (1 << 22, 1 << 20),
    )(encoder_table, encoder_shift, picks, *arrived)
    return encoded.transpose(2, 0, 1, 3)


def solution(mesh):
    return jax.shard_map(
        on_device,
        mesh=mesh,
        in_specs=(
            P(("grp", "tm"), "row", "col"),
            P("grp"),
            P(("grp", "tm"), "row", "col"),
            P(),
            P(),
            P(),
            P(),
        ),
        out_specs=P("grp", "row", "tm", "col"),
        check_vma=False,
    )
```

```python
import functools

import jax
import jax.numpy as jnp
from jax import lax
from jax.experimental import pallas as pl
from jax.experimental.pallas import tpu as pltpu
from jax.sharding import PartitionSpec as P

CH = 32
OUTC = 64
LANES = 128
PX = LANES // CH
F32 = jnp.float32
BF16 = jnp.bfloat16
VMEM = pltpu.VMEM
SMEM = pltpu.SMEM
DMA = pltpu.SemaphoreType.DMA


def up_to(value, step):
    return (value + step - 1) // step * step


def vm():
    return pl.BlockSpec(memory_space=pltpu.VMEM)


def far():
    return pl.BlockSpec(memory_space=pltpu.HBM)


def in_far(array):
    return pltpu.with_memory_space_constraint(array, pltpu.HBM)


def fetch(*pairs):
    *pairs, sems = pairs
    copies = [
        pltpu.make_async_copy(source, target, sems.at[i])
        for i, (source, target) in enumerate(pairs)
    ]
    for copy in copies:
        copy.start()
    return copies


def side(axis, toward):
    index = lax.axis_index(axis)
    if toward > 0:
        return index < lax.axis_size(axis) - 1
    return index > 0


def directions(axis):
    return (0,) if lax.axis_size(axis) <= 2 else (1, -1)


def halo_kernel(row_dirs, col_dirs, frames_far, valid_far, tile, *refs):
    sends, (frames, marks, valid, sems) = refs[:-4], refs[-4:]
    whole, flags = fetch((frames_far, frames), (valid_far, valid), sems)
    flags.wait()
    height = frames.shape[1]
    lanes = frames.shape[2]
    blocks = valid.shape[2]
    last = valid.shape[1] - 1
    wide = lanes // blocks
    if last + 1 < marks.shape[0]:
        marks[...] = jnp.zeros(marks.shape, F32)
    for line in range(last + 1):
        for block in range(blocks):
            marks[line : line + 1, block * wide : (block + 1) * wide] = jnp.full(
                (1, wide), valid[0, line, block].astype(F32), F32
            )
    tile[0, height:, :] = marks[...].astype(BF16)
    whole.wait()
    tile[0, :height, :] = frames[0]
    spots = lax.broadcasted_iota(jnp.int32, (4, lanes), 0)
    tail = frames[0, height - 8 : height, :].astype(F32)[4:8]
    head = frames[0, 0:8, :].astype(F32)[0:4]
    down = jnp.where(spots == 0, marks[last : last + 1, :], tail)
    upper = jnp.where(spots == 3, marks[0:1, :], head)
    bands = {1: down, -1: upper}
    bands[0] = jnp.where(side("row", 1), down, upper)
    columns = {}
    for way, first, block in ((1, lanes - LANES, blocks - 1), (-1, 0, 0)):
        edge = frames[0, :, first : first + LANES].astype(F32)
        flags = jnp.concatenate(
            [
                jnp.full((8, LANES), valid[0, line, block].astype(F32), F32)
                for line in range(last + 1)
            ],
            axis=0,
        )
        columns[way] = jnp.concatenate([edge, flags], axis=0)
    columns[0] = jnp.where(side("col", 1), columns[1], columns[-1])
    outs = iter(sends)
    for way in row_dirs:
        next(outs)[...] = bands[way].astype(BF16)
    for way in col_dirs:
        next(outs)[...] = columns[way].astype(BF16)
    for row_way in row_dirs:
        for col_way in col_dirs:
            right = bands[row_way][:, lanes - LANES :]
            left = bands[row_way][:, :LANES]
            if col_way == 0:
                picked = jnp.where(side("col", 1), right, left)
            else:
                picked = right if col_way > 0 else left
            next(outs)[...] = picked.astype(BF16)


def turned(weight, staged):
    count = LANES // weight.shape[0]
    values = weight[...].astype(F32)
    staged[:, : values.shape[1]] = jnp.concatenate([values] * count, axis=0)
    return jnp.concatenate(
        [
            jnp.transpose(staged[:, first : first + LANES])
            for first in range(0, staged.shape[1], LANES)
        ],
        axis=0,
    )


def prepare_kernel(sources, *refs):
    far_refs, refs = refs[:5], refs[5:]
    filter_outs, encoder_outs, refs = refs[:2], refs[2:5], refs[5:]
    near_refs, (filter_staged, encoder_staged, sems) = refs[:5], refs[5:]
    copies = fetch(*zip(far_refs, near_refs), sems)
    for copy in copies:
        copy.wait()
    filter_matrix(*filter_outs, *near_refs[:2], filter_staged)
    encoder_matrix(sources, *encoder_outs, *near_refs[2:], encoder_staged)


def filter_matrix(out, shift, weight, bias, staged):
    shift[...] = jnp.broadcast_to(jnp.concatenate([bias[...]] * PX, axis=1), shift.shape)
    tiled = turned(weight, staged)
    taps = {
        (dy, dx): tiled[(3 * dy + dx) * CH : (3 * dy + dx + 1) * CH]
        for dy in range(3)
        for dx in range(3)
    }
    lane = lax.broadcasted_iota(jnp.int32, (CH, LANES), 1)
    line = lax.broadcasted_iota(jnp.int32, (CH, LANES), 0)
    nothing = jnp.zeros((CH, LANES), F32)
    for q in range(4):
        cell = []
        for v in range(4):
            terms = [
                taps[q - a, v - b]
                for a in range(2)
                for b in range(2)
                if 0 <= q - a < 3 and 0 <= v - b < 3
            ]
            cell.append(functools.reduce(jnp.add, terms) * 0.25)
        for u in range(-1, 2 * PX + 1):
            filt = nothing
            for p in range(PX):
                if 0 <= u - 2 * p + 1 < 4:
                    filt = jnp.where(lane // CH == p, cell[u - 2 * p + 1], filt)
            mean = nothing
            if 0 <= u < 2 * PX and q in (1, 2):
                mean = jnp.where(lane == u // 2 * CH + line, 0.25, nothing)
            spot = {-1: 2 * LANES + LANES - CH, 2 * PX: 2 * LANES}.get(u, u * CH)
            spot += q * 3 * LANES
            out[spot : spot + CH, :LANES] = filt.astype(BF16)
            out[spot : spot + CH, LANES:] = mean.astype(BF16)
        spot = q * 3 * LANES + 2 * LANES + CH
        out[spot : spot + LANES - 2 * CH, :] = jnp.zeros((LANES - 2 * CH, 2 * LANES), BF16)


def encoder_matrix(sources, out, shift, picks, weight, bias, owner, staged):
    shift[...] = jnp.broadcast_to(jnp.concatenate([bias[...]] * PX, axis=1), shift.shape)
    me = lax.axis_index("tm")
    for spot, source in enumerate(sources):
        time = jnp.full(picks.shape[1:], owner[source(me)], jnp.int32)
        picks[spot] = time
    double = turned(weight, staged)
    lane = lax.broadcasted_iota(jnp.int32, (CH, LANES), 1)
    nothing = jnp.zeros((CH, LANES), F32)
    wide = PX * OUTC
    for lag in range(3):
        for dy in range(3):
            base = (lag * 9 + dy * 3) * CH

            def tap(dx):
                if 0 <= dx < 3:
                    return double[base + dx * CH : base + (dx + 1) * CH]
                return nothing

            for u in range(-1, PX + 1):
                spot = {-1: 2 * LANES - CH, PX: LANES}.get(u, u * CH) + dy * 2 * LANES
                for half in range(PX // 2):
                    value = jnp.where(
                        lane < OUTC, tap(u - 2 * half + 1), tap(u - 2 * half)
                    )
                    first = lag * wide + half * LANES
                    out[spot : spot + CH, first : first + LANES] = value.astype(BF16)
            spot = dy * 2 * LANES + LANES + CH
            out[spot : spot + LANES - 2 * CH, lag * wide : (lag + 1) * wide] = jnp.zeros(
                (LANES - 2 * CH, wide), BF16
            )


def pool_kernel(
    order, stride, crossed, tile, up, dn, rt, lf, ur, ul, dr, dl, matrix, bias, *refs
):
    outs, (x, pooled) = refs[:-2], refs[-2:]
    height = rt.shape[0] // 2
    lanes = tile.shape[2]
    groups = lanes // LANES
    blocks = groups // 2
    cells = groups // 2 + 1
    rows = height // 2
    held = pooled.shape[0] // outs[0].shape[1]
    has_up = side("row", -1).astype(F32)
    has_dn = side("row", 1).astype(F32)
    toward = -1 if crossed else 1
    has_rt = side("col", toward).astype(F32)
    has_lf = side("col", -toward).astype(F32)
    around = groups + 2
    pitch = x.shape[0] // around
    below = 8 + height
    blank = jnp.zeros((pitch - below, LANES), F32)
    right = rt[...].astype(F32) * has_rt
    left = lf[...].astype(F32) * has_lf
    for g in range(around):
        base = g * pitch
        window = pl.ds(g * LANES, LANES)
        if g < groups:
            own = tile[0, :height, window].astype(F32)
            over = up[:, window].astype(F32) * has_up
            under = dn[:, window].astype(F32) * has_dn
        elif g == groups:
            own = right[:height]
            over = ur[...].astype(F32) * (has_up * has_rt)
            under = dr[...].astype(F32) * (has_dn * has_rt)
        else:
            own = left[:height]
            over = ul[...].astype(F32) * (has_up * has_lf)
            under = dl[...].astype(F32) * (has_dn * has_lf)
        x[base : base + 4, :] = jnp.zeros((4, LANES), F32)
        x[base + 4 : base + 8, :] = over
        x[base + 8 : base + below, :] = own
        x[base + below : base + pitch, :] = blank
        x[base + below : base + below + 4, :] = under

    lane = lax.broadcasted_iota(jnp.int32, (held, LANES), 1)
    spot = lax.broadcasted_iota(jnp.int32, (held, LANES), 0)
    pieces = []
    for q in range(4):
        strips = [
            x[pl.ds(g * pitch + 5 + q, held, stride=2), :] for g in range(around)
        ]
        pieces.append(jnp.concatenate([strips[2 * c] for c in range(cells)], axis=0))
        pieces.append(jnp.concatenate([strips[2 * c + 1] for c in range(cells)], axis=0))
        pieces.append(
            jnp.concatenate(
                [
                    jnp.where(
                        lane < LANES // 2,
                        strips[(2 * c + 2) % around],
                        strips[(2 * c - 1) % around],
                    )
                    for c in range(cells)
                ],
                axis=0,
            )
        )
    patches = jnp.concatenate([piece.astype(BF16) for piece in pieces], axis=1)
    result = jnp.dot(patches, matrix[...], preferred_element_type=F32)
    shift = bias[0:1, :]
    for c in range(cells):
        mask = jnp.zeros((held, LANES), F32)
        if c < blocks:
            base = 2 * c * pitch
            above = x[base + 4 : base + 5, :]
            under = x[base + below + 3 : base + below + 4, :]
            marks = tile[0, height:, 2 * c * LANES : (2 * c + 1) * LANES].astype(F32)
            inside = [marks[line : line + 1] for line in range(height // 8)]
        else:
            one = lax.broadcasted_iota(jnp.int32, (1, LANES), 1) < LANES // 2

            def both(line):
                first = groups * pitch + line
                second = first + pitch
                return jnp.where(one, x[first : first + 1, :], x[second : second + 1, :])

            above, under = both(4), both(below + 3)
            inside = [
                jnp.where(
                    one,
                    right[height + 8 * line : height + 8 * line + 1],
                    left[height + 8 * line : height + 8 * line + 1],
                )
                for line in range(height // 8)
            ]
        mask = jnp.where(spot == 0, above, mask)
        mask = jnp.where(spot == rows + 1, under, mask)
        for line, value in enumerate(inside):
            mask = jnp.where((spot >= 1 + 4 * line) & (spot < 5 + 4 * line), value, mask)
        part = result[c * held : (c + 1) * held]
        pooled[c * held : (c + 1) * held, :] = part[:, LANES:] + mask * (part[:, :LANES] + shift)
    me = lax.axis_index("tm")
    for out, step in zip(outs, order):
        band = step(me)
        for dy in range(stride + 2):
            out[dy] = pooled[pl.ds(band * stride + dy, out.shape[1], stride=held), :].astype(BF16)


def encode_kernel(matrix, bias, picks, *refs):
    arrived, (out, chunks, folded) = refs[:-3], refs[-3:]
    frames = chunks.shape[0]
    if len(arrived) == frames:
        pieces = [piece[...].astype(F32) for piece in arrived]
    else:
        pieces = [arrived[0][slot].astype(F32) for slot in range(frames)]
    lines = pieces[0].shape[0]
    for t in range(frames):
        for dy in range(lines):
            chosen = pieces[0][dy]
            for slot in range(1, frames):
                chosen = jnp.where(picks[slot] == t, pieces[slot][dy], chosen)
            chunks[t, dy] = chosen
    cells = out.shape[3] // (PX * OUTC)
    stride = out.shape[1]
    held = chunks.shape[2]
    kept = up_to(cells, 8)
    lane = lax.broadcasted_iota(jnp.int32, (kept, LANES), 1)
    wide = PX * OUTC
    shift = bias[0:1, :]
    pitch = folded.shape[1] // kept
    for line in range(stride):
        lines = []
        for dy in range(3):
            now, beside = [], []
            for t in range(frames):
                full = chunks[t, line + dy]
                ahead = pltpu.roll(full, held - 1, 0)
                behind = pltpu.roll(full, 1, 0)
                first = lax.broadcasted_iota(jnp.int32, (held, LANES), 0) == 0
                behind = jnp.where(first, full[cells : cells + 1], behind)
                now.append(full[:kept])
                beside.append(jnp.where(lane < LANES // 2, ahead[:kept], behind[:kept]))
            lines.append(jnp.concatenate(now, axis=0).astype(BF16))
            lines.append(jnp.concatenate(beside, axis=0).astype(BF16))
        patches = jnp.concatenate(lines, axis=1)
        result = jnp.dot(patches, matrix[...], preferred_element_type=F32)
        for j in range(frames - 1):
            total = shift
            for lag in range(3):
                t = max(j + 1 - lag, 0)
                total = total + result[t * kept : (t + 1) * kept, lag * wide : (lag + 1) * wide]
            for half in range(wide // LANES):
                folded[half, pl.ds(j, kept, stride=pitch), :] = total[
                    :, half * LANES : (half + 1) * LANES
                ]
        for g in range(cells):
            for half in range(wide // LANES):
                first = g * wide + half * LANES
                out[0, line, :, first : first + LANES] = folded[
                    half, g * pitch : g * pitch + frames - 1, :
                ].astype(BF16)


def ring(axis, shift):
    count = lax.axis_size(axis)
    return [(i, i + shift) for i in range(count) if 0 <= i + shift < count]


def pairs_of(axis, way):
    count = lax.axis_size(axis)
    if way == 0:
        return [(i, count - 1 - i) for i in range(count)]
    return ring(axis, way)


def call(kernel, outs, specs, scratch, work=(0, 0), limit=16):
    return pl.pallas_call(
        kernel,
        out_shape=outs,
        in_specs=specs,
        out_specs=jax.tree.map(lambda _: vm(), outs),
        scratch_shapes=scratch,
        compiler_params=pltpu.CompilerParams(vmem_limit_bytes=limit << 20),
        cost_estimate=pl.CostEstimate(flops=work[0], bytes_accessed=work[1], transcendentals=0),
    )


def on_device(
    frames, owner_map, valid_blocks, deblock_weight, deblock_bias, encoder_weight, encoder_bias
):
    height = frames.shape[1]
    lanes = frames.shape[2]
    bands = lax.axis_size("tm")
    shaped = jax.ShapeDtypeStruct
    row_dirs, col_dirs = directions("row"), directions("col")
    n_col = lax.axis_size("col")
    direct = bands <= 4
    crossed = direct and n_col == 2
    marked = up_to(height // 8, 8)

    band = shaped((4, lanes), BF16)
    column = shaped((2 * height, LANES), BF16)
    corner = shaped((4, LANES), BF16)
    tile, *sends = call(
        functools.partial(halo_kernel, row_dirs, col_dirs),
        [shaped((1, height + marked, lanes), BF16)]
        + [band] * len(row_dirs)
        + [column] * len(col_dirs)
        + [corner] * (len(row_dirs) * len(col_dirs)),
        [far(), far()],
        [
            VMEM(frames.shape, BF16),
            VMEM((marked, lanes), F32),
            SMEM(valid_blocks.shape, jnp.int32),
            DMA((2,)),
        ],
    )(in_far(frames), in_far(valid_blocks))
    sends = iter(sends)
    by_row, by_col, by_both = {}, {}, {}
    flip = [(0, 1), (1, 0)]

    def product(first, second):
        return [(a * n_col + c, b * n_col + d) for a, b in first for c, d in second]

    for w in row_dirs:
        if crossed:
            pairs = product(pairs_of("row", w), flip)
            by_row[w] = lax.ppermute(next(sends), ("row", "col"), pairs)
        else:
            by_row[w] = lax.ppermute(next(sends), "row", pairs_of("row", w))
    for v in col_dirs:
        if crossed:
            by_col[v] = next(sends)
            tile = lax.ppermute(tile, "col", flip)
        else:
            by_col[v] = lax.ppermute(next(sends), "col", pairs_of("col", v))
    for w in row_dirs:
        for v in col_dirs:
            if crossed:
                by_both[w, v] = lax.ppermute(next(sends), "row", pairs_of("row", w))
            else:
                pairs = product(pairs_of("row", w), pairs_of("col", v))
                by_both[w, v] = lax.ppermute(next(sends), ("row", "col"), pairs)

    def pick(table, way):
        return table[way] if way in table else table[0]

    def pick_both(w, v):
        return by_both[w if w in row_dirs else 0, v if v in col_dirs else 0]

    rows = height // 2
    stride = rows // bands
    cells = lanes // LANES // 2 + 1
    held = up_to(rows + 2, 8)
    kept = up_to(cells, 8)
    piece = shaped((stride + 2, kept, LANES), BF16)
    if direct:
        order = [functools.partial(lambda k, me: lax.rem(me + k, bands), k) for k in range(bands)]
        sources = [
            functools.partial(lambda k, me: lax.rem(me + bands - k, bands), k)
            for k in range(bands)
        ]
    else:
        order = [functools.partial(lambda k, me: k, k) for k in range(bands)]
        sources = order
    filter_table, filter_shift, encoder_table, encoder_shift, picks = call(
        functools.partial(prepare_kernel, sources),
        [
            shaped((12 * LANES, 2 * LANES), BF16),
            shaped((8, LANES), F32),
            shaped((6 * LANES, 3 * PX * OUTC), BF16),
            shaped((8, PX * OUTC), F32),
            shaped((bands, kept, LANES), jnp.int32),
        ],
        [far()] * 5,
        [
            VMEM((CH, 9 * CH), BF16),
            VMEM((1, CH), F32),
            VMEM((OUTC, 27 * CH), BF16),
            VMEM((1, OUTC), F32),
            SMEM(owner_map.shape, jnp.int32),
            VMEM((LANES, up_to(9 * CH, LANES)), F32),
            VMEM((LANES, up_to(27 * CH, LANES)), F32),
            DMA((5,)),
        ],
        (1 << 22, 1 << 20),
    )(
        in_far(deblock_weight.T),
        in_far(deblock_bias.reshape(1, CH)),
        in_far(encoder_weight.T),
        in_far(encoder_bias.reshape(1, OUTC)),
        in_far(owner_map),
    )
    parts = call(
        functools.partial(pool_kernel, order, stride, crossed),
        [piece] * bands,
        [vm()] * 11,
        [
            VMEM(((lanes // LANES + 2) * up_to(8 + 2 * held, 8), LANES), F32),
            VMEM((kept * held, LANES), F32),
        ],
        (1 << 22, 1 << 20),
    )(
        tile,
        pick(by_row, 1),
        pick(by_row, -1),
        pick(by_col, -1),
        pick(by_col, 1),
        pick_both(1, -1),
        pick_both(1, 1),
        pick_both(-1, -1),
        pick_both(-1, 1),
        filter_table,
        filter_shift,
    )
    if direct:
        arrived = []
        for k in range(bands):
            shift = [(i, (i + k) % bands) for i in range(bands)]
            if crossed:
                pairs = product(shift, flip)
                arrived.append(lax.ppermute(parts[k], ("tm", "col"), pairs))
            elif k:
                arrived.append(lax.ppermute(parts[k], "tm", shift))
            else:
                arrived.append(parts[k])
    else:
        arrived = [
            lax.all_to_all(jnp.stack(parts), "tm", split_axis=0, concat_axis=0, tiled=True)
        ]
    encoded = call(
        encode_kernel,
        shaped((1, stride, bands - 1, lanes // 2 // CH * OUTC), BF16),
        [vm()] * (3 + len(arrived)),
        [
            VMEM((bands, stride + 2, kept, LANES), F32),
            VMEM((PX * OUTC // LANES, kept * up_to(bands - 1, 8), LANES), F32),
        ],
        (1 << 22, 1 << 20),
    )(encoder_table, encoder_shift, picks, *arrived)
    return encoded.transpose(2, 0, 1, 3)


def solution(mesh):
    return jax.shard_map(
        on_device,
        mesh=mesh,
        in_specs=(
            P(("grp", "tm"), "row", "col"),
            P("grp"),
            P(("grp", "tm"), "row", "col"),
            P(),
            P(),
            P(),
            P(),
        ),
        out_specs=P("grp", "row", "tm", "col"),
        check_vma=False,
    )
```

```python
import functools

import jax
import jax.numpy as jnp
from jax import lax
from jax.experimental import pallas as pl
from jax.experimental.pallas import tpu as pltpu
from jax.sharding import PartitionSpec as P

CH = 32
OUTC = 64
LANES = 128
PX = LANES // CH
F32 = jnp.float32
BF16 = jnp.bfloat16
VMEM = pltpu.VMEM
SMEM = pltpu.SMEM
DMA = pltpu.SemaphoreType.DMA


def up_to(value, step):
    return (value + step - 1) // step * step


def vm():
    return pl.BlockSpec(memory_space=pltpu.VMEM)


def far():
    return pl.BlockSpec(memory_space=pltpu.HBM)


def in_far(array):
    return pltpu.with_memory_space_constraint(array, pltpu.HBM)


def fetch(*pairs):
    *pairs, sems = pairs
    copies = [
        pltpu.make_async_copy(source, target, sems.at[i])
        for i, (source, target) in enumerate(pairs)
    ]
    for copy in copies:
        copy.start()
    return copies


def side(axis, toward):
    index = lax.axis_index(axis)
    if toward > 0:
        return index < lax.axis_size(axis) - 1
    return index > 0


def directions(axis):
    return (0,) if lax.axis_size(axis) <= 2 else (1, -1)


def halo_kernel(row_dirs, col_dirs, crossed, frames_far, valid_far, *refs):
    sends, (frames, marks, valid, sems) = refs[:-4], refs[-4:]
    whole, flags = fetch((frames_far, frames), (valid_far, valid), sems)
    flags.wait()
    height = frames.shape[1]
    lanes = frames.shape[2]
    blocks = valid.shape[2]
    last = valid.shape[1] - 1
    wide = lanes // blocks
    for block in range(blocks):
        window = pl.ds(block * wide, wide)
        for spot, line in ((0, last), (3, 0)):
            marks[spot : spot + 1, window] = jnp.full(
                (1, wide), valid[0, line, block].astype(F32), F32
            )
    whole.wait()
    spots = lax.broadcasted_iota(jnp.int32, (4, lanes), 0)
    tail = frames[0, height - 8 : height, :].astype(F32)[4:8]
    head = frames[0, 0:8, :].astype(F32)[0:4]
    down = jnp.where(spots == 0, marks[0:1, :], tail)
    upper = jnp.where(spots == 3, marks[3:4, :], head)
    bands = {1: down, -1: upper}
    bands[0] = jnp.where(side("row", 1), down, upper)
    columns = {}
    for way, first, block in ((1, lanes - LANES, blocks - 1), (-1, 0, 0)):
        edge = frames[0, :, first : first + LANES].astype(F32)
        flags = jnp.concatenate(
            [
                jnp.full((8, LANES), valid[0, line, block].astype(F32), F32)
                for line in range(last + 1)
            ],
            axis=0,
        )
        columns[way] = jnp.concatenate([edge, flags], axis=0)
    columns[0] = jnp.where(side("col", 1), columns[1], columns[-1])
    outs = iter(sends)
    for way in row_dirs:
        next(outs)[...] = bands[way].astype(BF16)
    for way in col_dirs:
        next(outs)[...] = columns[way].astype(BF16)
    for row_way in () if crossed else row_dirs:
        for col_way in col_dirs:
            right = bands[row_way][:, lanes - LANES :]
            left = bands[row_way][:, :LANES]
            if col_way == 0:
                picked = jnp.where(side("col", 1), right, left)
            else:
                picked = right if col_way > 0 else left
            next(outs)[...] = picked.astype(BF16)


def corner_kernel(row_dirs, frames, valid, *refs):
    count = len(row_dirs)
    bands, outs = refs[:count], refs[count:]
    height = frames.shape[1]
    lanes = frames.shape[2]
    first = side("col", 1)
    flags = valid[0].astype(F32)
    blocks = flags.shape[1]
    lane = lax.broadcasted_iota(jnp.int32, (1, blocks), 1)
    wanted = jnp.where(first, 0, blocks - 1)

    def mark(line):
        row = jnp.where(lane == wanted, flags[line : line + 1], 0.0)
        return jnp.broadcast_to(jnp.sum(row, axis=1, keepdims=True), (4, LANES))

    def edge(start):
        left = frames[0, start : start + 8, :LANES].astype(F32)
        right = frames[0, start : start + 8, lanes - LANES :].astype(F32)
        return jnp.where(first, left, right)

    spots = lax.broadcasted_iota(jnp.int32, (4, LANES), 0)
    down = jnp.where(spots == 0, mark(flags.shape[0] - 1), edge(height - 8)[4:8])
    upper = jnp.where(spots == 3, mark(0), edge(0)[0:4])
    corners = {1: down, -1: upper, 0: jnp.where(side("row", 1), down, upper)}
    for way, band, out in zip(row_dirs, bands, outs):
        out[:, :lanes] = band[...]
        out[:, lanes:] = corners[way].astype(BF16)


def turned(weight, staged):
    count = LANES // weight.shape[0]
    values = weight[...].astype(F32)
    staged[:, : values.shape[1]] = jnp.concatenate([values] * count, axis=0)
    return jnp.concatenate(
        [
            jnp.transpose(staged[:, first : first + LANES])
            for first in range(0, staged.shape[1], LANES)
        ],
        axis=0,
    )


def prepare_kernel(held, sources, *refs):
    far_refs, refs = refs[:6], refs[6:]
    filter_outs, encoder_outs, refs = refs[:3], refs[3:6], refs[6:]
    near_refs, (filter_staged, encoder_staged, sems) = refs[:6], refs[6:]
    copies = fetch(*zip(far_refs, near_refs), sems)
    for copy in copies:
        copy.wait()
    filter_matrix(held, *filter_outs, *near_refs[:3], filter_staged)
    encoder_matrix(sources, *encoder_outs, *near_refs[3:], encoder_staged)


def filter_matrix(held, out, shift, masks, weight, bias, valid, staged):
    shift[...] = jnp.broadcast_to(jnp.concatenate([bias[...]] * PX, axis=1), shift.shape)
    spots = lax.broadcasted_iota(jnp.int32, (held, LANES), 0)
    for c in range(valid.shape[2]):
        mask = jnp.zeros((held, LANES), F32)
        for line in range(valid.shape[1]):
            inside = (spots >= 1 + 4 * line) & (spots < 5 + 4 * line)
            mask = jnp.where(inside, valid[0, line, c].astype(F32), mask)
        masks[c * held : (c + 1) * held, :] = mask
    tiled = turned(weight, staged)
    taps = {
        (dy, dx): tiled[(3 * dy + dx) * CH : (3 * dy + dx + 1) * CH]
        for dy in range(3)
        for dx in range(3)
    }
    lane = lax.broadcasted_iota(jnp.int32, (CH, LANES), 1)
    line = lax.broadcasted_iota(jnp.int32, (CH, LANES), 0)
    nothing = jnp.zeros((CH, LANES), F32)
    for q in range(4):
        cell = []
        for v in range(4):
            terms = [
                taps[q - a, v - b]
                for a in range(2)
                for b in range(2)
                if 0 <= q - a < 3 and 0 <= v - b < 3
            ]
            cell.append(functools.reduce(jnp.add, terms) * 0.25)
        for u in range(-1, 2 * PX + 1):
            filt = nothing
            for p in range(PX):
                if 0 <= u - 2 * p + 1 < 4:
                    filt = jnp.where(lane // CH == p, cell[u - 2 * p + 1], filt)
            mean = nothing
            if 0 <= u < 2 * PX and q in (1, 2):
                mean = jnp.where(lane == u // 2 * CH + line, 0.25, nothing)
            spot = {-1: 2 * LANES + LANES - CH, 2 * PX: 2 * LANES}.get(u, u * CH)
            spot += q * 3 * LANES
            out[spot : spot + CH, :LANES] = filt.astype(BF16)
            out[spot : spot + CH, LANES:] = mean.astype(BF16)
        spot = q * 3 * LANES + 2 * LANES + CH
        out[spot : spot + LANES - 2 * CH, :] = jnp.zeros((LANES - 2 * CH, 2 * LANES), BF16)


def encoder_matrix(sources, out, shift, picks, weight, bias, owner, staged):
    shift[...] = jnp.broadcast_to(jnp.concatenate([bias[...]] * PX, axis=1), shift.shape)
    me = lax.axis_index("tm")
    for spot, source in enumerate(sources):
        time = jnp.full(picks.shape[1:], owner[source(me)], jnp.int32)
        picks[spot] = time
    double = turned(weight, staged)
    lane = lax.broadcasted_iota(jnp.int32, (CH, LANES), 1)
    nothing = jnp.zeros((CH, LANES), F32)
    wide = PX * OUTC
    for lag in range(3):
        for dy in range(3):
            base = (lag * 9 + dy * 3) * CH

            def tap(dx):
                if 0 <= dx < 3:
                    return double[base + dx * CH : base + (dx + 1) * CH]
                return nothing

            for u in range(-1, PX + 1):
                spot = {-1: 2 * LANES - CH, PX: LANES}.get(u, u * CH) + dy * 2 * LANES
                for half in range(PX // 2):
                    value = jnp.where(
                        lane < OUTC, tap(u - 2 * half + 1), tap(u - 2 * half)
                    )
                    first = lag * wide + half * LANES
                    out[spot : spot + CH, first : first + LANES] = value.astype(BF16)
            spot = dy * 2 * LANES + LANES + CH
            out[spot : spot + LANES - 2 * CH, lag * wide : (lag + 1) * wide] = jnp.zeros(
                (LANES - 2 * CH, wide), BF16
            )


def pool_kernel(
    order, stride, crossed, tile, matrix, bias, masks, up, dn, rt, lf, *refs
):
    if not crossed:
        (ur, ul, dr, dl), refs = refs[:4], refs[4:]
    outs, (x, pooled) = refs[:-2], refs[-2:]
    height = rt.shape[0] // 2
    lanes = tile.shape[2]
    groups = lanes // LANES
    blocks = groups // 2
    cells = groups // 2 + 1
    rows = height // 2
    held = pooled.shape[0] // outs[0].shape[1]
    has_up = side("row", -1).astype(F32)
    has_dn = side("row", 1).astype(F32)
    if crossed:
        ur = ul = up.at[:, lanes : lanes + LANES]
        dr = dl = dn.at[:, lanes : lanes + LANES]
    toward = -1 if crossed else 1
    has_rt = side("col", toward).astype(F32)
    has_lf = side("col", -toward).astype(F32)
    around = groups + 2
    pitch = x.shape[0] // around
    below = 8 + height
    blank = jnp.zeros((pitch - below, LANES), F32)
    right = rt[...].astype(F32) * has_rt
    left = lf[...].astype(F32) * has_lf
    for g in range(around):
        base = g * pitch
        window = pl.ds(g * LANES, LANES)
        if g < groups:
            own = tile[0, :height, window].astype(F32)
            over = up[:, window].astype(F32) * has_up
            under = dn[:, window].astype(F32) * has_dn
        elif g == groups:
            own = right[:height]
            over = ur[...].astype(F32) * (has_up * has_rt)
            under = dr[...].astype(F32) * (has_dn * has_rt)
        else:
            own = left[:height]
            over = ul[...].astype(F32) * (has_up * has_lf)
            under = dl[...].astype(F32) * (has_dn * has_lf)
        x[base : base + 4, :] = jnp.zeros((4, LANES), F32)
        x[base + 4 : base + 8, :] = over
        x[base + 8 : base + below, :] = own
        x[base + below : base + pitch, :] = blank
        x[base + below : base + below + 4, :] = under

    lane = lax.broadcasted_iota(jnp.int32, (held, LANES), 1)
    spot = lax.broadcasted_iota(jnp.int32, (held, LANES), 0)
    pieces = []
    for q in range(4):
        strips = [
            x[pl.ds(g * pitch + 5 + q, held, stride=2), :] for g in range(around)
        ]
        pieces.append(jnp.concatenate([strips[2 * c] for c in range(cells)], axis=0))
        pieces.append(jnp.concatenate([strips[2 * c + 1] for c in range(cells)], axis=0))
        pieces.append(
            jnp.concatenate(
                [
                    jnp.where(
                        lane < LANES // 2,
                        strips[(2 * c + 2) % around],
                        strips[(2 * c - 1) % around],
                    )
                    for c in range(cells)
                ],
                axis=0,
            )
        )
    patches = jnp.concatenate([piece.astype(BF16) for piece in pieces], axis=1)
    result = jnp.dot(patches, matrix[...], preferred_element_type=F32)
    shift = bias[0:1, :]
    for c in range(cells):
        mask = jnp.zeros((held, LANES), F32)
        if c < blocks:
            base = 2 * c * pitch
            above = x[base + 4 : base + 5, :]
            under = x[base + below + 3 : base + below + 4, :]
            mask = masks[c * held : (c + 1) * held, :]
            inside = []
        else:
            one = lax.broadcasted_iota(jnp.int32, (1, LANES), 1) < LANES // 2

            def both(line):
                first = groups * pitch + line
                second = first + pitch
                return jnp.where(one, x[first : first + 1, :], x[second : second + 1, :])

            above, under = both(4), both(below + 3)
            inside = [
                jnp.where(
                    one,
                    right[height + 8 * line : height + 8 * line + 1],
                    left[height + 8 * line : height + 8 * line + 1],
                )
                for line in range(height // 8)
            ]
        mask = jnp.where(spot == 0, above, mask)
        mask = jnp.where(spot == rows + 1, under, mask)
        for line, value in enumerate(inside):
            mask = jnp.where((spot >= 1 + 4 * line) & (spot < 5 + 4 * line), value, mask)
        part = result[c * held : (c + 1) * held]
        pooled[c * held : (c + 1) * held, :] = part[:, LANES:] + mask * (part[:, :LANES] + shift)
    me = lax.axis_index("tm")
    for out, step in zip(outs, order):
        band = step(me)
        for dy in range(stride + 2):
            out[dy] = pooled[pl.ds(band * stride + dy, out.shape[1], stride=held), :].astype(BF16)


def encode_kernel(matrix, bias, picks, *refs):
    arrived, (out, chunks, folded) = refs[:-3], refs[-3:]
    frames = chunks.shape[0]
    if len(arrived) == frames:
        pieces = [piece[...].astype(F32) for piece in arrived]
    else:
        pieces = [arrived[0][slot].astype(F32) for slot in range(frames)]
    lines = pieces[0].shape[0]
    for t in range(frames):
        for dy in range(lines):
            chosen = pieces[0][dy]
            for slot in range(1, frames):
                chosen = jnp.where(picks[slot] == t, pieces[slot][dy], chosen)
            chunks[t, dy] = chosen
    cells = out.shape[3] // (PX * OUTC)
    stride = out.shape[1]
    held = chunks.shape[2]
    kept = up_to(cells, 8)
    lane = lax.broadcasted_iota(jnp.int32, (kept, LANES), 1)
    wide = PX * OUTC
    shift = bias[0:1, :]
    pitch = folded.shape[1] // kept
    for line in range(stride):
        lines = []
        for dy in range(3):
            now, beside = [], []
            for t in range(frames):
                full = chunks[t, line + dy]
                ahead = pltpu.roll(full, held - 1, 0)
                behind = pltpu.roll(full, 1, 0)
                first = lax.broadcasted_iota(jnp.int32, (held, LANES), 0) == 0
                behind = jnp.where(first, full[cells : cells + 1], behind)
                now.append(full[:kept])
                beside.append(jnp.where(lane < LANES // 2, ahead[:kept], behind[:kept]))
            lines.append(jnp.concatenate(now, axis=0).astype(BF16))
            lines.append(jnp.concatenate(beside, axis=0).astype(BF16))
        patches = jnp.concatenate(lines, axis=1)
        result = jnp.dot(patches, matrix[...], preferred_element_type=F32)
        for j in range(frames - 1):
            total = shift
            for lag in range(3):
                t = max(j + 1 - lag, 0)
                total = total + result[t * kept : (t + 1) * kept, lag * wide : (lag + 1) * wide]
            for half in range(wide // LANES):
                folded[half, pl.ds(j, kept, stride=pitch), :] = total[
                    :, half * LANES : (half + 1) * LANES
                ]
        for g in range(cells):
            for half in range(wide // LANES):
                first = g * wide + half * LANES
                out[0, line, :, first : first + LANES] = folded[
                    half, g * pitch : g * pitch + frames - 1, :
                ].astype(BF16)


def ring(axis, shift):
    count = lax.axis_size(axis)
    return [(i, i + shift) for i in range(count) if 0 <= i + shift < count]


def pairs_of(axis, way):
    count = lax.axis_size(axis)
    if way == 0:
        return [(i, count - 1 - i) for i in range(count)]
    return ring(axis, way)


def call(kernel, outs, specs, scratch, work=(0, 0), limit=16):
    return pl.pallas_call(
        kernel,
        out_shape=outs,
        in_specs=specs,
        out_specs=jax.tree.map(lambda _: vm(), outs),
        scratch_shapes=scratch,
        compiler_params=pltpu.CompilerParams(vmem_limit_bytes=limit << 20),
        cost_estimate=pl.CostEstimate(flops=work[0], bytes_accessed=work[1], transcendentals=0),
    )


def on_device(
    frames, owner_map, valid_blocks, deblock_weight, deblock_bias, encoder_weight, encoder_bias
):
    height = frames.shape[1]
    lanes = frames.shape[2]
    bands = lax.axis_size("tm")
    shaped = jax.ShapeDtypeStruct
    row_dirs, col_dirs = directions("row"), directions("col")
    n_col = lax.axis_size("col")
    direct = bands <= 4
    crossed = direct and n_col == 2

    band = shaped((4, lanes), BF16)
    column = shaped((2 * height, LANES), BF16)
    corner = shaped((4, LANES), BF16)
    tile, flags = frames, in_far(valid_blocks)
    flip = [(0, 1), (1, 0)]

    def product(first, second):
        return [(a * n_col + c, b * n_col + d) for a, b in first for c, d in second]

    if crossed:
        tile = lax.ppermute(frames, "col", flip)
        flags = lax.ppermute(valid_blocks, "col", flip)
    sends = call(
        functools.partial(halo_kernel, row_dirs, col_dirs, crossed),
        [band] * len(row_dirs)
        + [column] * len(col_dirs)
        + [corner] * (0 if crossed else len(row_dirs) * len(col_dirs)),
        [far(), far()],
        [
            VMEM(frames.shape, BF16),
            VMEM((8, lanes), F32),
            SMEM(valid_blocks.shape, jnp.int32),
            DMA((2,)),
        ],
    )(in_far(frames), in_far(valid_blocks))
    row_sends, sends = sends[: len(row_dirs)], iter(sends[len(row_dirs) :])
    if crossed:
        row_sends = call(
            functools.partial(corner_kernel, row_dirs),
            [shaped((4, lanes + LANES), BF16)] * len(row_dirs),
            [vm()] * (2 + len(row_dirs)),
            [],
        )(tile, flags, *row_sends)
    by_row, by_col, by_both = {}, {}, {}
    for w, send in zip(row_dirs, row_sends):
        if crossed:
            pairs = product(pairs_of("row", w), flip)
            by_row[w] = lax.ppermute(send, ("row", "col"), pairs)
        else:
            by_row[w] = lax.ppermute(send, "row", pairs_of("row", w))
    for v in col_dirs:
        by_col[v] = next(sends)
        if not crossed:
            by_col[v] = lax.ppermute(by_col[v], "col", pairs_of("col", v))
    for w, v in () if crossed else [(w, v) for w in row_dirs for v in col_dirs]:
        pairs = product(pairs_of("row", w), pairs_of("col", v))
        by_both[w, v] = lax.ppermute(next(sends), ("row", "col"), pairs)

    def pick(table, way):
        return table[way] if way in table else table[0]

    def pick_both(w, v):
        return by_both[w if w in row_dirs else 0, v if v in col_dirs else 0]

    rows = height // 2
    stride = rows // bands
    cells = lanes // LANES // 2 + 1
    held = up_to(rows + 2, 8)
    kept = up_to(cells, 8)
    piece = shaped((stride + 2, kept, LANES), BF16)
    if direct:
        order = [functools.partial(lambda k, me: lax.rem(me + k, bands), k) for k in range(bands)]
        sources = [
            functools.partial(lambda k, me: lax.rem(me + bands - k, bands), k)
            for k in range(bands)
        ]
    else:
        order = [functools.partial(lambda k, me: k, k) for k in range(bands)]
        sources = order
    filter_table, filter_shift, masks, encoder_table, encoder_shift, picks = call(
        functools.partial(prepare_kernel, held, sources),
        [
            shaped((12 * LANES, 2 * LANES), BF16),
            shaped((8, LANES), F32),
            shaped(((cells - 1) * held, LANES), F32),
            shaped((6 * LANES, 3 * PX * OUTC), BF16),
            shaped((8, PX * OUTC), F32),
            shaped((bands, kept, LANES), jnp.int32),
        ],
        [far(), far(), vm() if crossed else far(), far(), far(), far()],
        [
            VMEM((CH, 9 * CH), BF16),
            VMEM((1, CH), F32),
            SMEM(valid_blocks.shape, jnp.int32),
            VMEM((OUTC, 27 * CH), BF16),
            VMEM((1, OUTC), F32),
            SMEM(owner_map.shape, jnp.int32),
            VMEM((LANES, up_to(9 * CH, LANES)), F32),
            VMEM((LANES, up_to(27 * CH, LANES)), F32),
            DMA((6,)),
        ],
        (1 << 22, 1 << 20),
    )(
        in_far(deblock_weight.T),
        in_far(deblock_bias.reshape(1, CH)),
        flags,
        in_far(encoder_weight.T),
        in_far(encoder_bias.reshape(1, OUTC)),
        in_far(owner_map),
    )
    around = [pick(by_row, 1), pick(by_row, -1), pick(by_col, -1), pick(by_col, 1)]
    if not crossed:
        around += [pick_both(w, v) for w in (1, -1) for v in (-1, 1)]
    parts = call(
        functools.partial(pool_kernel, order, stride, crossed),
        [piece] * bands,
        [vm()] * (4 + len(around)),
        [
            VMEM(((lanes // LANES + 2) * up_to(8 + 2 * held, 8), LANES), F32),
            VMEM((kept * held, LANES), F32),
        ],
        (1 << 22, 1 << 20),
    )(tile, filter_table, filter_shift, masks, *around)
    if direct:
        arrived = []
        for k in range(bands):
            shift = [(i, (i + k) % bands) for i in range(bands)]
            if crossed:
                pairs = product(shift, flip)
                arrived.append(lax.ppermute(parts[k], ("tm", "col"), pairs))
            elif k:
                arrived.append(lax.ppermute(parts[k], "tm", shift))
            else:
                arrived.append(parts[k])
    else:
        arrived = [
            lax.all_to_all(jnp.stack(parts), "tm", split_axis=0, concat_axis=0, tiled=True)
        ]
    encoded = call(
        encode_kernel,
        shaped((1, stride, bands - 1, lanes // 2 // CH * OUTC), BF16),
        [vm()] * (3 + len(arrived)),
        [
            VMEM((bands, stride + 2, kept, LANES), F32),
            VMEM((PX * OUTC // LANES, kept * up_to(bands - 1, 8), LANES), F32),
        ],
        (1 << 22, 1 << 20),
    )(encoder_table, encoder_shift, picks, *arrived)
    return encoded.transpose(2, 0, 1, 3)


def solution(mesh):
    return jax.shard_map(
        on_device,
        mesh=mesh,
        in_specs=(
            P(("grp", "tm"), "row", "col"),
            P("grp"),
            P(("grp", "tm"), "row", "col"),
            P(),
            P(),
            P(),
            P(),
        ),
        out_specs=P("grp", "row", "tm", "col"),
        check_vma=False,
    )
```

```python
import functools

import jax
import jax.numpy as jnp
from jax import lax
from jax.experimental import pallas as pl
from jax.experimental.pallas import tpu as pltpu
from jax.sharding import PartitionSpec as P

CH = 32
OUTC = 64
LANES = 128
PX = LANES // CH
F32 = jnp.float32
BF16 = jnp.bfloat16
VMEM = pltpu.VMEM
SMEM = pltpu.SMEM
DMA = pltpu.SemaphoreType.DMA


def up_to(value, step):
    return (value + step - 1) // step * step


def vm():
    return pl.BlockSpec(memory_space=pltpu.VMEM)


def far():
    return pl.BlockSpec(memory_space=pltpu.HBM)


def in_far(array):
    return pltpu.with_memory_space_constraint(array, pltpu.HBM)


def fetch(*pairs):
    *pairs, sems = pairs
    copies = [
        pltpu.make_async_copy(source, target, sems.at[i])
        for i, (source, target) in enumerate(pairs)
    ]
    for copy in copies:
        copy.start()
    return copies


def side(axis, toward):
    index = lax.axis_index(axis)
    if toward > 0:
        return index < lax.axis_size(axis) - 1
    return index > 0


def directions(axis):
    return (0,) if lax.axis_size(axis) <= 2 else (1, -1)


def halo_kernel(row_dirs, col_dirs, crossed, frames_far, valid_far, *refs):
    sends, (frames, marks, valid, sems) = refs[:-4], refs[-4:]
    whole, flags = fetch((frames_far, frames), (valid_far, valid), sems)
    flags.wait()
    height = frames.shape[1]
    lanes = frames.shape[2]
    blocks = valid.shape[2]
    last = valid.shape[1] - 1
    wide = lanes // blocks
    for block in range(blocks):
        window = pl.ds(block * wide, wide)
        for spot, line in ((0, last), (3, 0)):
            marks[spot : spot + 1, window] = jnp.full(
                (1, wide), valid[0, line, block].astype(F32), F32
            )
    whole.wait()
    spots = lax.broadcasted_iota(jnp.int32, (4, lanes), 0)
    tail = frames[0, height - 8 : height, :].astype(F32)[4:8]
    head = frames[0, 0:8, :].astype(F32)[0:4]
    down = jnp.where(spots == 0, marks[0:1, :], tail)
    upper = jnp.where(spots == 3, marks[3:4, :], head)
    bands = {1: down, -1: upper}
    bands[0] = jnp.where(side("row", 1), down, upper)
    columns = {}
    for way, first, block in ((1, lanes - LANES, blocks - 1), (-1, 0, 0)):
        edge = frames[0, :, first : first + LANES].astype(F32)
        flags = jnp.concatenate(
            [
                jnp.full((8, LANES), valid[0, line, block].astype(F32), F32)
                for line in range(last + 1)
            ],
            axis=0,
        )
        columns[way] = jnp.concatenate([edge, flags], axis=0)
    columns[0] = jnp.where(side("col", 1), columns[1], columns[-1])
    outs = iter(sends)
    for way in row_dirs:
        next(outs)[...] = bands[way].astype(BF16)
    for way in col_dirs:
        next(outs)[...] = columns[way].astype(BF16)
    for row_way in () if crossed else row_dirs:
        for col_way in col_dirs:
            right = bands[row_way][:, lanes - LANES :]
            left = bands[row_way][:, :LANES]
            if col_way == 0:
                picked = jnp.where(side("col", 1), right, left)
            else:
                picked = right if col_way > 0 else left
            next(outs)[...] = picked.astype(BF16)


def corner_kernel(row_dirs, frames, valid, *refs):
    count = len(row_dirs)
    bands, outs = refs[:count], refs[count:]
    height = frames.shape[1]
    lanes = frames.shape[2]
    first = side("col", 1)
    flags = valid[0].astype(F32)
    blocks = flags.shape[1]
    lane = lax.broadcasted_iota(jnp.int32, (1, blocks), 1)
    wanted = jnp.where(first, 0, blocks - 1)

    def mark(line):
        row = jnp.where(lane == wanted, flags[line : line + 1], 0.0)
        return jnp.broadcast_to(jnp.sum(row, axis=1, keepdims=True), (4, LANES))

    def edge(start):
        left = frames[0, start : start + 8, :LANES].astype(F32)
        right = frames[0, start : start + 8, lanes - LANES :].astype(F32)
        return jnp.where(first, left, right)

    spots = lax.broadcasted_iota(jnp.int32, (4, LANES), 0)
    down = jnp.where(spots == 0, mark(flags.shape[0] - 1), edge(height - 8)[4:8])
    upper = jnp.where(spots == 3, mark(0), edge(0)[0:4])
    corners = {1: down, -1: upper, 0: jnp.where(side("row", 1), down, upper)}
    for way, band, out in zip(row_dirs, bands, outs):
        out[:, :lanes] = band[...]
        out[:, lanes:] = corners[way].astype(BF16)


def turned(weight, staged):
    count = LANES // weight.shape[0]
    values = weight[...].astype(F32)
    staged[:, : values.shape[1]] = jnp.concatenate([values] * count, axis=0)
    return jnp.concatenate(
        [
            jnp.transpose(staged[:, first : first + LANES])
            for first in range(0, staged.shape[1], LANES)
        ],
        axis=0,
    )


def prepare_kernel(held, sources, *refs):
    far_refs, refs = refs[:6], refs[6:]
    filter_outs, encoder_outs, refs = refs[:3], refs[3:6], refs[6:]
    near_refs, (filter_staged, encoder_staged, sems) = refs[:6], refs[6:]
    copies = fetch(*zip(far_refs, near_refs), sems)
    for copy in copies:
        copy.wait()
    filter_matrix(held, *filter_outs, *near_refs[:3], filter_staged)
    encoder_matrix(sources, *encoder_outs, *near_refs[3:], encoder_staged)


def filter_matrix(held, out, shift, masks, weight, bias, valid, staged):
    shift[...] = jnp.broadcast_to(jnp.concatenate([bias[...]] * PX, axis=1), shift.shape)
    spots = lax.broadcasted_iota(jnp.int32, (held, LANES), 0)
    for c in range(valid.shape[2]):
        mask = jnp.zeros((held, LANES), F32)
        for line in range(valid.shape[1]):
            inside = (spots >= 1 + 4 * line) & (spots < 5 + 4 * line)
            mask = jnp.where(inside, valid[0, line, c].astype(F32), mask)
        masks[c * held : (c + 1) * held, :] = mask
    tiled = turned(weight, staged)
    taps = {
        (dy, dx): tiled[(3 * dy + dx) * CH : (3 * dy + dx + 1) * CH]
        for dy in range(3)
        for dx in range(3)
    }
    lane = lax.broadcasted_iota(jnp.int32, (CH, LANES), 1)
    line = lax.broadcasted_iota(jnp.int32, (CH, LANES), 0)
    nothing = jnp.zeros((CH, LANES), F32)
    for q in range(4):
        cell = []
        for v in range(4):
            terms = [
                taps[q - a, v - b]
                for a in range(2)
                for b in range(2)
                if 0 <= q - a < 3 and 0 <= v - b < 3
            ]
            cell.append(functools.reduce(jnp.add, terms) * 0.25)
        for u in range(-1, 2 * PX + 1):
            filt = nothing
            for p in range(PX):
                if 0 <= u - 2 * p + 1 < 4:
                    filt = jnp.where(lane // CH == p, cell[u - 2 * p + 1], filt)
            mean = nothing
            if 0 <= u < 2 * PX and q in (1, 2):
                mean = jnp.where(lane == u // 2 * CH + line, 0.25, nothing)
            spot = {-1: 2 * LANES + LANES - CH, 2 * PX: 2 * LANES}.get(u, u * CH)
            spot += q * 3 * LANES
            out[spot : spot + CH, :LANES] = filt.astype(BF16)
            out[spot : spot + CH, LANES:] = mean.astype(BF16)
        spot = q * 3 * LANES + 2 * LANES + CH
        out[spot : spot + LANES - 2 * CH, :] = jnp.zeros((LANES - 2 * CH, 2 * LANES), BF16)


def encoder_matrix(sources, out, shift, picks, weight, bias, owner, staged):
    shift[...] = jnp.broadcast_to(jnp.concatenate([bias[...]] * PX, axis=1), shift.shape)
    me = lax.axis_index("tm")
    for spot, source in enumerate(sources):
        time = jnp.full(picks.shape[1:], owner[source(me)], jnp.int32)
        picks[spot] = time
    double = turned(weight, staged)
    lane = lax.broadcasted_iota(jnp.int32, (CH, LANES), 1)
    nothing = jnp.zeros((CH, LANES), F32)
    wide = PX * OUTC
    for lag in range(3):
        for dy in range(3):
            base = (lag * 9 + dy * 3) * CH

            def tap(dx):
                if 0 <= dx < 3:
                    return double[base + dx * CH : base + (dx + 1) * CH]
                return nothing

            for u in range(-1, PX + 1):
                spot = {-1: 2 * LANES - CH, PX: LANES}.get(u, u * CH) + dy * 2 * LANES
                for half in range(PX // 2):
                    value = jnp.where(
                        lane < OUTC, tap(u - 2 * half + 1), tap(u - 2 * half)
                    )
                    first = lag * wide + half * LANES
                    out[spot : spot + CH, first : first + LANES] = value.astype(BF16)
            spot = dy * 2 * LANES + LANES + CH
            out[spot : spot + LANES - 2 * CH, lag * wide : (lag + 1) * wide] = jnp.zeros(
                (LANES - 2 * CH, wide), BF16
            )


def pool_kernel(
    order, stride, crossed, tile, matrix, bias, masks, up, dn, rt, lf, *refs
):
    if not crossed:
        (ur, ul, dr, dl), refs = refs[:4], refs[4:]
    outs, (x, pooled) = refs[:-2], refs[-2:]
    height = rt.shape[0] // 2
    lanes = tile.shape[2]
    groups = lanes // LANES
    blocks = groups // 2
    cells = groups // 2 + 1
    rows = height // 2
    held = pooled.shape[0] // outs[0].shape[1]
    has_up = side("row", -1).astype(F32)
    has_dn = side("row", 1).astype(F32)
    if crossed:
        ur = ul = up.at[:, lanes : lanes + LANES]
        dr = dl = dn.at[:, lanes : lanes + LANES]
    toward = -1 if crossed else 1
    has_rt = side("col", toward).astype(F32)
    has_lf = side("col", -toward).astype(F32)
    around = groups + 2
    pitch = x.shape[0] // around
    below = 8 + height
    right = rt[...].astype(F32) * has_rt
    left = lf[...].astype(F32) * has_lf
    for g in range(around):
        base = g * pitch
        window = pl.ds(g * LANES, LANES)
        if g < groups:
            own = tile[0, :height, window].astype(F32)
            over = up[:, window].astype(F32) * has_up
            under = dn[:, window].astype(F32) * has_dn
        elif g == groups:
            own = right[:height]
            over = ur[...].astype(F32) * (has_up * has_rt)
            under = dr[...].astype(F32) * (has_dn * has_rt)
        else:
            own = left[:height]
            over = ul[...].astype(F32) * (has_up * has_lf)
            under = dl[...].astype(F32) * (has_dn * has_lf)
        x[base + 4 : base + 8, :] = over
        x[base + 8 : base + below, :] = own
        x[base + below : base + below + 4, :] = under

    lane = lax.broadcasted_iota(jnp.int32, (held, LANES), 1)
    spot = lax.broadcasted_iota(jnp.int32, (held, LANES), 0)
    pieces = []
    for q in range(4):
        strips = [
            x[pl.ds(g * pitch + 5 + q, held, stride=2), :] for g in range(around)
        ]
        pieces.append(jnp.concatenate([strips[2 * c] for c in range(cells)], axis=0))
        pieces.append(jnp.concatenate([strips[2 * c + 1] for c in range(cells)], axis=0))
        pieces.append(
            jnp.concatenate(
                [
                    jnp.where(
                        lane < LANES // 2,
                        strips[(2 * c + 2) % around],
                        strips[(2 * c - 1) % around],
                    )
                    for c in range(cells)
                ],
                axis=0,
            )
        )
    patches = jnp.concatenate([piece.astype(BF16) for piece in pieces], axis=1)
    result = jnp.dot(patches, matrix[...], preferred_element_type=F32)
    shift = bias[0:1, :]
    for c in range(cells):
        mask = jnp.zeros((held, LANES), F32)
        if c < blocks:
            base = 2 * c * pitch
            above = x[base + 4 : base + 5, :]
            under = x[base + below + 3 : base + below + 4, :]
            mask = masks[c * held : (c + 1) * held, :]
            inside = []
        else:
            one = lax.broadcasted_iota(jnp.int32, (1, LANES), 1) < LANES // 2

            def both(line):
                first = groups * pitch + line
                second = first + pitch
                return jnp.where(one, x[first : first + 1, :], x[second : second + 1, :])

            above, under = both(4), both(below + 3)
            inside = [
                jnp.where(
                    one,
                    right[height + 8 * line : height + 8 * line + 1],
                    left[height + 8 * line : height + 8 * line + 1],
                )
                for line in range(height // 8)
            ]
        mask = jnp.where(spot == 0, above, mask)
        mask = jnp.where(spot == rows + 1, under, mask)
        for line, value in enumerate(inside):
            mask = jnp.where((spot >= 1 + 4 * line) & (spot < 5 + 4 * line), value, mask)
        part = result[c * held : (c + 1) * held]
        pooled[c * held : (c + 1) * held, :] = part[:, LANES:] + mask * (part[:, :LANES] + shift)
    me = lax.axis_index("tm")
    for out, step in zip(outs, order):
        band = step(me)
        for dy in range(stride + 2):
            out[dy] = pooled[pl.ds(band * stride + dy, out.shape[1], stride=held), :].astype(BF16)


def encode_kernel(matrix, bias, picks, *refs):
    arrived, (out, chunks, folded) = refs[:-3], refs[-3:]
    frames = chunks.shape[0]
    if len(arrived) == frames:
        pieces = [piece[...].astype(F32) for piece in arrived]
    else:
        pieces = [arrived[0][slot].astype(F32) for slot in range(frames)]
    lines = pieces[0].shape[0]
    for t in range(frames):
        for dy in range(lines):
            chosen = pieces[0][dy]
            for slot in range(1, frames):
                chosen = jnp.where(picks[slot] == t, pieces[slot][dy], chosen)
            chunks[t, dy] = chosen
    cells = out.shape[3] // (PX * OUTC)
    stride = out.shape[1]
    held = chunks.shape[2]
    kept = up_to(cells, 8)
    lane = lax.broadcasted_iota(jnp.int32, (kept, LANES), 1)
    wide = PX * OUTC
    shift = bias[0:1, :]
    pitch = folded.shape[1] // kept
    for line in range(stride):
        lines = []
        for dy in range(3):
            now, beside = [], []
            for t in range(frames):
                full = chunks[t, line + dy]
                ahead = pltpu.roll(full, held - 1, 0)
                behind = pltpu.roll(full, 1, 0)
                first = lax.broadcasted_iota(jnp.int32, (held, LANES), 0) == 0
                behind = jnp.where(first, full[cells : cells + 1], behind)
                now.append(full[:kept])
                beside.append(jnp.where(lane < LANES // 2, ahead[:kept], behind[:kept]))
            lines.append(jnp.concatenate(now, axis=0).astype(BF16))
            lines.append(jnp.concatenate(beside, axis=0).astype(BF16))
        patches = jnp.concatenate(lines, axis=1)
        result = jnp.dot(patches, matrix[...], preferred_element_type=F32)
        for j in range(frames - 1):
            total = shift
            for lag in range(3):
                t = max(j + 1 - lag, 0)
                total = total + result[t * kept : (t + 1) * kept, lag * wide : (lag + 1) * wide]
            for half in range(wide // LANES):
                folded[half, pl.ds(j, kept, stride=pitch), :] = total[
                    :, half * LANES : (half + 1) * LANES
                ]
        for g in range(cells):
            for half in range(wide // LANES):
                first = g * wide + half * LANES
                out[0, line, :, first : first + LANES] = folded[
                    half, g * pitch : g * pitch + frames - 1, :
                ].astype(BF16)


def window_of(piece, line, cells):
    held = piece.shape[1]
    kept = up_to(cells, 8)
    lane = lax.broadcasted_iota(jnp.int32, (kept, LANES), 1)
    first = lax.broadcasted_iota(jnp.int32, (held, LANES), 0) == 0
    lines = []
    for dy in range(3):
        full = piece[line + dy].astype(F32)
        ahead = pltpu.roll(full, held - 1, 0)
        behind = jnp.where(first, full[cells : cells + 1], pltpu.roll(full, 1, 0))
        lines.append(full[:kept])
        lines.append(jnp.where(lane < LANES // 2, ahead[:kept], behind[:kept]))
    return jnp.concatenate(lines, axis=1)


def gathered(total, result, pick, j, half):
    for lag in range(3):
        first = lag * PX * OUTC + half * LANES
        part = result[:, first : first + LANES]
        total = total + jnp.where(pick == max(j + 1 - lag, 0), part, 0.0)
    return total


def early_kernel(cells, matrix, bias, picks, *refs):
    arrived, sums = refs[:-1], refs[-1]
    kept = sums.shape[2]
    for line in range(sums.shape[0]):
        patches = jnp.concatenate([window_of(piece, line, cells) for piece in arrived], axis=0)
        result = jnp.dot(patches.astype(BF16), matrix[...], preferred_element_type=F32)
        results = [result[slot * kept : (slot + 1) * kept] for slot in range(len(arrived))]
        for j in range(sums.shape[1]):
            for half in range(PX * OUTC // LANES):
                lanes = pl.ds(half * LANES, LANES)
                total = jnp.broadcast_to(bias[0:1, lanes], (kept, LANES))
                for slot, result in enumerate(results):
                    total = gathered(total, result, picks[slot], j, half)
                sums[line, j, :, lanes] = total


def late_kernel(cells, matrix, picks, sums, piece, out, folded):
    kept = sums.shape[2]
    wide = PX * OUTC
    pitch = folded.shape[1] // kept
    pick = picks[picks.shape[0] - 1]
    count = sums.shape[1]
    for line in range(sums.shape[0]):
        patches = window_of(piece, line, cells)
        result = jnp.dot(patches.astype(BF16), matrix[...], preferred_element_type=F32)
        for j in range(count):
            for half in range(wide // LANES):
                before = sums[line, j, :, half * LANES : (half + 1) * LANES]
                folded[half, pl.ds(j, kept, stride=pitch), :] = gathered(
                    before, result, pick, j, half
                )
        for g in range(cells):
            for half in range(wide // LANES):
                first = g * wide + half * LANES
                out[0, line, :, first : first + LANES] = folded[
                    half, g * pitch : g * pitch + count, :
                ].astype(BF16)


def ring(axis, shift):
    count = lax.axis_size(axis)
    return [(i, i + shift) for i in range(count) if 0 <= i + shift < count]


def pairs_of(axis, way):
    count = lax.axis_size(axis)
    if way == 0:
        return [(i, count - 1 - i) for i in range(count)]
    return ring(axis, way)


def call(kernel, outs, specs, scratch, work=(0, 0), limit=16):
    return pl.pallas_call(
        kernel,
        out_shape=outs,
        in_specs=specs,
        out_specs=jax.tree.map(lambda _: vm(), outs),
        scratch_shapes=scratch,
        compiler_params=pltpu.CompilerParams(vmem_limit_bytes=limit << 20),
        cost_estimate=pl.CostEstimate(flops=work[0], bytes_accessed=work[1], transcendentals=0),
    )


def on_device(
    frames, owner_map, valid_blocks, deblock_weight, deblock_bias, encoder_weight, encoder_bias
):
    height = frames.shape[1]
    lanes = frames.shape[2]
    bands = lax.axis_size("tm")
    shaped = jax.ShapeDtypeStruct
    row_dirs, col_dirs = directions("row"), directions("col")
    n_col = lax.axis_size("col")
    direct = bands <= 4
    crossed = direct and n_col == 2

    band = shaped((4, lanes), BF16)
    column = shaped((2 * height, LANES), BF16)
    corner = shaped((4, LANES), BF16)
    tile, flags = frames, in_far(valid_blocks)
    flip = [(0, 1), (1, 0)]

    def product(first, second):
        return [(a * n_col + c, b * n_col + d) for a, b in first for c, d in second]

    if crossed:
        tile = lax.ppermute(frames, "col", flip)
        flags = lax.ppermute(valid_blocks, "col", flip)
    sends = call(
        functools.partial(halo_kernel, row_dirs, col_dirs, crossed),
        [band] * len(row_dirs)
        + [column] * len(col_dirs)
        + [corner] * (0 if crossed else len(row_dirs) * len(col_dirs)),
        [far(), far()],
        [
            VMEM(frames.shape, BF16),
            VMEM((8, lanes), F32),
            SMEM(valid_blocks.shape, jnp.int32),
            DMA((2,)),
        ],
    )(in_far(frames), in_far(valid_blocks))
    row_sends, sends = sends[: len(row_dirs)], iter(sends[len(row_dirs) :])
    if crossed:
        row_sends = call(
            functools.partial(corner_kernel, row_dirs),
            [shaped((4, lanes + LANES), BF16)] * len(row_dirs),
            [vm()] * (2 + len(row_dirs)),
            [],
        )(tile, flags, *row_sends)
    by_row, by_col, by_both = {}, {}, {}
    for w, send in zip(row_dirs, row_sends):
        if crossed:
            pairs = product(pairs_of("row", w), flip)
            by_row[w] = lax.ppermute(send, ("row", "col"), pairs)
        else:
            by_row[w] = lax.ppermute(send, "row", pairs_of("row", w))
    for v in col_dirs:
        by_col[v] = next(sends)
        if not crossed:
            by_col[v] = lax.ppermute(by_col[v], "col", pairs_of("col", v))
    for w, v in () if crossed else [(w, v) for w in row_dirs for v in col_dirs]:
        pairs = product(pairs_of("row", w), pairs_of("col", v))
        by_both[w, v] = lax.ppermute(next(sends), ("row", "col"), pairs)

    def pick(table, way):
        return table[way] if way in table else table[0]

    def pick_both(w, v):
        return by_both[w if w in row_dirs else 0, v if v in col_dirs else 0]

    rows = height // 2
    stride = rows // bands
    cells = lanes // LANES // 2 + 1
    held = up_to(rows + 2, 8)
    kept = up_to(cells, 8)
    piece = shaped((stride + 2, kept, LANES), BF16)
    if direct:
        order = [functools.partial(lambda k, me: lax.rem(me + k, bands), k) for k in range(bands)]
        sources = [
            functools.partial(lambda k, me: lax.rem(me + bands - k, bands), k)
            for k in range(bands)
        ]
    else:
        order = [functools.partial(lambda k, me: k, k) for k in range(bands)]
        sources = order
    filter_table, filter_shift, masks, encoder_table, encoder_shift, picks = call(
        functools.partial(prepare_kernel, held, sources),
        [
            shaped((12 * LANES, 2 * LANES), BF16),
            shaped((8, LANES), F32),
            shaped(((cells - 1) * held, LANES), F32),
            shaped((6 * LANES, 3 * PX * OUTC), BF16),
            shaped((8, PX * OUTC), F32),
            shaped((bands, kept, LANES), jnp.int32),
        ],
        [far(), far(), vm() if crossed else far(), far(), far(), far()],
        [
            VMEM((CH, 9 * CH), BF16),
            VMEM((1, CH), F32),
            SMEM(valid_blocks.shape, jnp.int32),
            VMEM((OUTC, 27 * CH), BF16),
            VMEM((1, OUTC), F32),
            SMEM(owner_map.shape, jnp.int32),
            VMEM((LANES, up_to(9 * CH, LANES)), F32),
            VMEM((LANES, up_to(27 * CH, LANES)), F32),
            DMA((6,)),
        ],
        (1 << 22, 1 << 20),
    )(
        in_far(deblock_weight.T),
        in_far(deblock_bias.reshape(1, CH)),
        flags,
        in_far(encoder_weight.T),
        in_far(encoder_bias.reshape(1, OUTC)),
        in_far(owner_map),
    )
    around = [pick(by_row, 1), pick(by_row, -1), pick(by_col, -1), pick(by_col, 1)]
    if not crossed:
        around += [pick_both(w, v) for w in (1, -1) for v in (-1, 1)]
    parts = call(
        functools.partial(pool_kernel, order, stride, crossed),
        [piece] * bands,
        [vm()] * (4 + len(around)),
        [
            VMEM(((lanes // LANES + 2) * up_to(8 + 2 * held, 8), LANES), F32),
            VMEM((kept * held, LANES), F32),
        ],
        (1 << 22, 1 << 20),
    )(tile, filter_table, filter_shift, masks, *around)
    if direct:
        arrived = []
        for k in range(bands):
            shift = [(i, (i + k) % bands) for i in range(bands)]
            if crossed:
                pairs = product(shift, flip)
                arrived.append(lax.ppermute(parts[k], ("tm", "col"), pairs))
            elif k:
                arrived.append(lax.ppermute(parts[k], "tm", shift))
            else:
                arrived.append(parts[k])
    else:
        arrived = [
            lax.all_to_all(jnp.stack(parts), "tm", split_axis=0, concat_axis=0, tiled=True)
        ]
    result = shaped((1, stride, bands - 1, lanes // 2 // CH * OUTC), BF16)
    fold = VMEM((PX * OUTC // LANES, kept * up_to(bands - 1, 8), LANES), F32)
    if direct and bands > 1:
        rows_kept = up_to(cells - 1, 8)
        sums = call(
            functools.partial(early_kernel, cells - 1),
            shaped((stride, bands - 1, rows_kept, PX * OUTC), F32),
            [vm()] * (2 + bands),
            [],
            (1 << 22, 1 << 20),
        )(encoder_table, encoder_shift, picks, *arrived[:-1])
        encoded = call(
            functools.partial(late_kernel, cells - 1),
            result,
            [vm()] * 4,
            [fold],
            (1 << 22, 1 << 20),
        )(encoder_table, picks, sums, arrived[-1])
    else:
        encoded = call(
            encode_kernel,
            result,
            [vm()] * (3 + len(arrived)),
            [VMEM((bands, stride + 2, kept, LANES), F32), fold],
            (1 << 22, 1 << 20),
        )(encoder_table, encoder_shift, picks, *arrived)
    return encoded.transpose(2, 0, 1, 3)


def solution(mesh):
    return jax.shard_map(
        on_device,
        mesh=mesh,
        in_specs=(
            P(("grp", "tm"), "row", "col"),
            P("grp"),
            P(("grp", "tm"), "row", "col"),
            P(),
            P(),
            P(),
            P(),
        ),
        out_specs=P("grp", "row", "tm", "col"),
        check_vma=False,
    )
```
